32 devices in a mesh: gx: 8 (over y, x, core), gy: 4 (over z).
Axes of the slice: x: 2, y: 2, z: 4, core: 2. Of those that a mesh axis runs over, the one named last changes fastest.
Arguments:
- permeability: float32 [8192, 1024], P('gx', 'gy'), may hold values from 0.01 to 100
- basis: float32 [64, 8, 256, 256], P('gx', 'gy'), may hold values from 0 to 1, as said below
- support: int32 [64, 8, 256, 256], P('gx', 'gy'), may hold values from 0 to 1, as said below
Outputs:
- smoothed: float32 [64, 8, 256, 256], P('gx', 'gy')
The draws below stay inside these ranges and needn't reach their ends.
Inputs may be any that keep to these rules, and one draw needn't show every extreme that they name: support is 1 exactly on a rectangle of the box that contains the block's own 128 x 128 cells in its middle and reaches 32 to 64 cells past them on each side, cut to the grid. basis is positive where support is 1 and 0 elsewhere.
All inputs are finite; a program needn't handle non-finite values.
Results may differ from the reference program's by a relative error of at most 0.0003.
Values sent between devices are 32-bit elements; how exact they have to be, the bound alone decides.
A program may use at most 128 MiB of HBM per device.

```python
import math
import jax
import jax.numpy as jnp

B = 128
H = 64
ITERS = 2
NX = 8192
NY = 1024
NBX = 64
NBY = 8


def support_parts(key):
    sides = jax.random.randint(jax.random.fold_in(key, 11), (NBX, NBY, 4), H // 2, H + 1)
    offsets = jnp.arange(2 * B, dtype=jnp.int32)
    start_x = (jnp.arange(NBX, dtype=jnp.int32) * B - H)[:, None, None] + offsets[None, None, :]
    start_y = (jnp.arange(NBY, dtype=jnp.int32) * B - H)[None, :, None] + offsets[None, None, :]
    in_x = (offsets[None, None, :] >= H - sides[:, :, 0:1]) & (offsets[None, None, :] < H + B + sides[:, :, 1:2])
    in_x = in_x & (start_x >= 0) & (start_x < NX)
    in_y = (offsets[None, None, :] >= H - sides[:, :, 2:3]) & (offsets[None, None, :] < H + B + sides[:, :, 3:4])
    in_y = in_y & (start_y >= 0) & (start_y < NY)
    return (in_x[:, :, :, None] & in_y[:, :, None, :]).astype(jnp.int32)


def draw_support(key, part):
    return support_parts(key)


def draw_basis(key, part):
    inside = support_parts(key).astype(jnp.float32)
    shape = (NBX, NBY, 2 * B, 2 * B)
    values = jnp.exp(jax.random.uniform(jax.random.fold_in(key, 23), shape, jnp.float32, jnp.log(0.05), 0.0))
    return values * inside


def levels(own_key, extent, pieces, smallest, top_value):
    loudness = 1.0
    for position, shards_of in pieces:
        draws = jax.random.uniform(jax.random.fold_in(jax.random.fold_in(own_key, 6), position), (shards_of,), jnp.float32, smallest / len(pieces), top_value / len(pieces))
        loudness = loudness * jnp.repeat(jnp.exp(draws), extent[position] // shards_of).reshape((-1,) + (1,) * (len(extent) - 1 - position))
    return loudness


def setup_inputs(seed: int = 0) -> dict:
    streams_of = jax.random.split(jax.random.key(seed), 4)
    return {
        "permeability": jnp.clip(jnp.exp(math.log(100.0) - 9.2103404 * jax.random.uniform(streams_of[0], (NX, NY), jnp.float32) ** levels(streams_of[0], (NX, NY), ((0, 8), (1, 4)), -0.2, 0.2)), 0.01, 100.0),
        "basis": draw_basis(jax.random.fold_in(streams_of[3], 71), 0),
        "support": draw_support(jax.random.fold_in(streams_of[3], 71), 0),
    }


relaxation = 2.0 / 3.0


def to_boxes(extended, count_x, count_y, block):
    tiles = extended.reshape(count_x + 1, block, count_y + 1, block).transpose(0, 2, 1, 3)
    upper = jnp.concatenate([tiles[:-1, :-1], tiles[:-1, 1:]], axis=3)
    lower = jnp.concatenate([tiles[1:, :-1], tiles[1:, 1:]], axis=3)
    return jnp.concatenate([upper, lower], axis=2)


def from_boxes(boxes, block):
    count_x, count_y = boxes.shape[0], boxes.shape[1]
    none = (0, 0)
    tiles = jnp.pad(boxes[:, :, :block, :block], ((0, 1), (0, 1), none, none))
    tiles = tiles + jnp.pad(boxes[:, :, :block, block:], ((0, 1), (1, 0), none, none))
    tiles = tiles + jnp.pad(boxes[:, :, block:, :block], ((1, 0), (0, 1), none, none))
    tiles = tiles + jnp.pad(boxes[:, :, block:, block:], ((1, 0), (1, 0), none, none))
    return tiles.transpose(0, 2, 1, 3).reshape((count_x + 1) * block, (count_y + 1) * block)


def harmonic(left, right):
    summed = left + right
    inside = summed > 0
    return jnp.where(inside, 2.0 * left * right / jnp.where(inside, summed, 1.0), 0.0)


def couplings(padded):
    faces_x = harmonic(padded[:-1, 1:-1], padded[1:, 1:-1])
    faces_y = harmonic(padded[1:-1, :-1], padded[1:-1, 1:])
    east = faces_x[1:]
    west = faces_x[:-1]
    north = faces_y[:, 1:]
    south = faces_y[:, :-1]
    diagonal = east + west + north + south
    return east, west, north, south, jnp.where(diagonal > 0, diagonal, 1.0)


def smooth(basis, support, east, west, north, south, diagonal):
    none = (0, 0)
    from_east = jnp.pad(basis[:, :, 1:, :], (none, none, (0, 1), none))
    from_west = jnp.pad(basis[:, :, :-1, :], (none, none, (1, 0), none))
    from_north = jnp.pad(basis[:, :, :, 1:], (none, none, none, (0, 1)))
    from_south = jnp.pad(basis[:, :, :, :-1], (none, none, none, (1, 0)))
    coupled = east * from_east + west * from_west + north * from_north + south * from_south
    return jnp.where(support > 0, (1.0 - relaxation) * basis + relaxation * coupled / diagonal, 0.0)


def reference(permeability, basis, support):
    padded = jnp.pad(permeability, H + 1)
    weights = tuple(to_boxes(field, NBX, NBY, B) for field in couplings(padded))
    for step in range(ITERS):
        basis = smooth(basis, support, *weights)
        summed = from_boxes(basis, B)
        summed = jnp.where(summed > 0, summed, 1.0)
        basis = basis / to_boxes(summed, NBX, NBY, B)
    return basis
```

```python
import jax
import jax.numpy as jnp
from jax import lax
from jax.experimental import pallas as pl
from jax.experimental.pallas import tpu as pltpu
from jax.sharding import PartitionSpec as P

ITERS = 2
MESH = pl.DeviceIdType.MESH
relaxation = 2.0 / 3.0
PAD = 8
CH = 32


def pick(k, table):
    value = jnp.int32(table[-1])
    for n in range(len(table) - 2, -1, -1):
        value = jnp.where(k == n, table[n], value)
    return value


def completed(rows, count):
    done, out = set(), []
    for i in rows:
        done.add(i)
        new = [rb for rb in (i, i + 1) if 0 < rb < count and rb - 1 in done and rb in done]
        assert len(new) <= 1
        out.append(new[0] if new else -1)
    return out


def needed(rows):
    seen, out = set(), []
    for i in rows:
        new = [rb for rb in (i, i + 1) if rb not in seen]
        seen.update(new)
        out.append(new)
    return out


def make_kernel(nx, ny, size_x, size_y, half):
    full = 2 * half
    last = nx
    strips = ny + 1

    def kernel(*refs):
        (perm_h, basis_h, out_h,
         a, b, d, w, s, inv, lk, rz, rx, rec, got, px, pe, pk, pr, hk, hr,
         a_sem, p_sem, o_sem, zs_sem, zr_sem, xs_sem, xr_sem,
         ps_sem, pr_sem, hs_sem, hr_sem, rs_sem, rr_sem) = refs
        gx, gy = lax.axis_index("gx"), lax.axis_index("gy")
        has_up, has_down = gx > 0, gx < size_x - 1
        has_left, has_right = gy > 0, gy < size_y - 1
        up, down = (gx - 1, gy), (gx + 1, gy)
        left, right = (gx, gy - 1), (gx, gy + 1)
        z_sides = ((0, has_left, left), (1, has_right, right))
        x_sides = ((0, has_up, up), (1, has_down, down))

        rows_1 = list(range(2, nx - 2)) + [1, nx - 2, 0, nx - 1]
        rows_2 = list(range(3, nx - 3)) + [2, nx - 3, 1, nx - 2, 0, nx - 1]
        need_1, need_2 = needed(rows_1), needed(rows_2)
        ready_1, ready_2 = completed(rows_1, nx), completed(rows_2, nx)
        halo = half // 2 + PAD
        height = px.shape[0]
        length = height - 2 * halo
        hw = half // 2

        def a_copy(i):
            return pltpu.make_async_copy(basis_h.at[i], a.at[i + 1, :, pl.ds(PAD, full), :], a_sem.at[i])

        def row_copy(side, target):
            src = 0 if side == 0 else length - halo
            dst = height - halo if side == 0 else 0
            return pltpu.make_async_remote_copy(
                src_ref=perm_h.at[pl.ds(src, halo), :], dst_ref=px.at[pl.ds(dst, halo), :],
                send_sem=rs_sem.at[side], recv_sem=rr_sem.at[1 - side],
                device_id=target, device_id_type=MESH)

        def row_arrival(side, target):
            dst = 0 if side == 0 else height - halo
            return pltpu.make_async_remote_copy(
                src_ref=perm_h.at[pl.ds(0, halo), :], dst_ref=px.at[pl.ds(dst, halo), :],
                send_sem=rs_sem.at[side], recv_sem=rr_sem.at[side],
                device_id=target, device_id_type=MESH)

        def pk_copy(side, target, rb):
            return pltpu.make_async_remote_copy(
                src_ref=pk.at[side, rb], dst_ref=pr.at[1 - side, rb],
                send_sem=ps_sem.at[side, rb], recv_sem=pr_sem.at[1 - side, rb],
                device_id=target, device_id_type=MESH)

        def pk_arrival(side, target, rb):
            return pltpu.make_async_remote_copy(
                src_ref=pk.at[side, rb], dst_ref=pr.at[side, rb],
                send_sem=ps_sem.at[side, rb], recv_sem=pr_sem.at[side, rb],
                device_id=target, device_id_type=MESH)

        def hk_copy(side, target):
            return pltpu.make_async_remote_copy(
                src_ref=hk, dst_ref=hr.at[1 - side],
                send_sem=hs_sem.at[side], recv_sem=hr_sem.at[1 - side],
                device_id=target, device_id_type=MESH)

        def hk_arrival(side, target):
            return pltpu.make_async_remote_copy(
                src_ref=hk, dst_ref=hr.at[side],
                send_sem=hs_sem.at[side], recv_sem=hr_sem.at[side],
                device_id=target, device_id_type=MESH)

        def o_copy(i):
            return pltpu.make_async_copy(a.at[i + 1, :, pl.ds(PAD, full), :], out_h.at[i], o_sem.at[i])

        def z_copy(side, target, rb):
            strip = 0 if side == 0 else strips - 1
            return pltpu.make_async_remote_copy(
                src_ref=s.at[rb, strip], dst_ref=rz.at[1 - side, rb],
                send_sem=zs_sem.at[0, side, rb], recv_sem=zr_sem.at[0, 1 - side, rb],
                device_id=target, device_id_type=MESH)

        def z_arrival(side, target, rb):
            return pltpu.make_async_remote_copy(
                src_ref=s.at[rb, 0], dst_ref=rz.at[side, rb],
                send_sem=zs_sem.at[0, side, rb], recv_sem=zr_sem.at[0, side, rb],
                device_id=target, device_id_type=MESH)

        def x_copy(side, target):
            rb = 0 if side == 0 else last
            return pltpu.make_async_remote_copy(
                src_ref=s.at[rb], dst_ref=rx.at[1 - side],
                send_sem=xs_sem.at[0, side], recv_sem=xr_sem.at[0, 1 - side],
                device_id=target, device_id_type=MESH)

        def x_arrival(side, target):
            return pltpu.make_async_remote_copy(
                src_ref=s.at[0], dst_ref=rx.at[side],
                send_sem=xs_sem.at[0, side], recv_sem=xr_sem.at[0, side],
                device_id=target, device_id_type=MESH)

        def pair(rb, side):
            first = 0 if side == 0 else ny - 2
            return rec.at[rb, side, :, pl.ds(first, 2)]

        def e_copy(side, target, rb):
            return pltpu.make_async_remote_copy(
                src_ref=pair(rb, side), dst_ref=got.at[1 - side, rb],
                send_sem=zs_sem.at[1, side, rb], recv_sem=zr_sem.at[1, 1 - side, rb],
                device_id=target, device_id_type=MESH)

        def e_arrival(side, target, rb):
            return pltpu.make_async_remote_copy(
                src_ref=pair(rb, side), dst_ref=got.at[side, rb],
                send_sem=zs_sem.at[1, side, rb], recv_sem=zr_sem.at[1, side, rb],
                device_id=target, device_id_type=MESH)

        def c_copy(side, target):
            src, dst, part = (0, last, 1) if side == 0 else (last, 0, 0)
            return pltpu.make_async_remote_copy(
                src_ref=rec.at[src, :, part], dst_ref=rec.at[dst, :, part],
                send_sem=xs_sem.at[1, side], recv_sem=xr_sem.at[1, 1 - side],
                device_id=target, device_id_type=MESH)

        def c_arrival(side, target):
            rb, part = (0, 0) if side == 0 else (last, 1)
            return pltpu.make_async_remote_copy(
                src_ref=rec.at[rb, :, part], dst_ref=rec.at[rb, :, part],
                send_sem=xs_sem.at[1, side], recv_sem=xr_sem.at[1, side],
                device_id=target, device_id_type=MESH)

        barrier = pltpu.get_barrier_semaphore()
        for _, has, target in z_sides + x_sides:
            @pl.when(has)
            def _():
                pl.semaphore_signal(barrier, inc=1, device_id=target, device_id_type=MESH)

        own = pltpu.make_async_copy(perm_h, px.at[pl.ds(halo, length), :], p_sem)
        own.start()

        @pl.loop(0, nx)
        def _(k):
            a_copy(pick(k, rows_1)).start()

        edge = jnp.zeros((PAD, full), jnp.float32)
        blank = jnp.zeros((half, half), jnp.float32)

        @pl.loop(0, nx)
        def _(i):
            for j in range(ny):
                a[i + 1, j, 0:PAD, :] = edge
                a[i + 1, j, PAD + full:, :] = edge
                b[i + 1, j, 0:PAD, :] = edge
                b[i + 1, j, PAD + full:, :] = edge

        for buf in (a, b):
            for j in range(ny):
                buf[0, j, PAD + full:, :] = edge
                buf[nx + 1, j, 0:PAD, :] = edge
                for r in range(0, full, half):
                    buf[0, j, PAD + r:PAD + r + half, :] = jnp.zeros((half, full), jnp.float32)
                    buf[nx + 1, j, PAD + r:PAD + r + half, :] = jnp.zeros((half, full), jnp.float32)

        for side, has, _t in z_sides:
            @pl.when(jnp.logical_not(has))
            def _():
                @pl.loop(0, nx + 1)
                def _(rb):
                    rz[side, rb] = blank
                    got[side, rb] = jnp.zeros((2, 2, PAD, half), jnp.float32)
                    pr[side, rb] = jnp.zeros((hw + PAD, half), jnp.float32)
                hr[side] = jnp.zeros((2, PAD, half), jnp.float32)

        for side, has, _t in x_sides:
            @pl.when(jnp.logical_not(has))
            def _():
                lo = 0 if side == 0 else height - halo
                px[lo:lo + halo, :] = jnp.zeros((halo, full), jnp.float32)
                rb, part = (0, 0) if side == 0 else (last, 1)
                rec[rb, :, part] = jnp.zeros((2, ny, PAD, half), jnp.float32)

        lanes = lax.broadcasted_iota(jnp.int32, (CH, full), 1)
        not_last, not_first = lanes < full - 1, lanes > 0

        def smooth_row(i):
            for j in range(ny):
                for r in range(0, full, CH):
                    lo = PAD + r
                    rb = i + r // half
                    q = r % half

                    def weight(n):
                        return w[n, rb, q:q + CH, j * half:j * half + full]

                    x = a[i + 1, j, lo:lo + CH, :]
                    ahead = jnp.where(not_last, pltpu.roll(x, full - 1, 1), 0.0)
                    behind = jnp.where(not_first, pltpu.roll(x, 1, 1), 0.0)
                    new = (1.0 - relaxation) * x + weight(0) * a[i + 1, j, lo + 1:lo + 1 + CH, :]
                    new = new + weight(1) * a[i + 1, j, lo - 1:lo - 1 + CH, :]
                    new = new + weight(2) * ahead + weight(3) * behind
                    b[i + 1, j, lo:lo + CH, :] = jnp.where(x > 0, new, 0.0)

        def partial(rb):
            for c in range(strips):
                for r in range(0, half, CH):
                    total = None
                    for j, lane in ((c - 1, half), (c, 0)):
                        if 0 <= j < ny:
                            low = b[rb, j, PAD + half + r:PAD + half + r + CH, lane:lane + half]
                            high = b[rb + 1, j, PAD + r:PAD + r + CH, lane:lane + half]
                            term = low + high
                            total = term if total is None else total + term
                    s[rb, c, r:r + CH, :] = total

        def z_send(rb):
            for side, has, target in z_sides:
                @pl.when(has)
                def _():
                    z_copy(side, target, rb).start()

        def invert(rb):
            for side, has, target in z_sides:
                @pl.when(has)
                def _():
                    z_arrival(side, target, rb).wait_recv()
            for c in range(strips):
                for r in range(0, half, CH):
                    total = s[rb, c, r:r + CH, :]
                    if c == 0:
                        total = total + rz[0, rb, r:r + CH, :]
                    if c == strips - 1:
                        total = total + rz[1, rb, r:r + CH, :]
                    inv[rb, r:r + CH, c * half:(c + 1) * half] = 1.0 / jnp.where(total > 0, total, 1.0)

        def x_send(side):
            _, has, target = x_sides[side]

            @pl.when(has)
            def _():
                x_copy(side, target).start()

        def x_add(side):
            _, has, target = x_sides[side]
            rb = 0 if side == 0 else last

            @pl.when(has)
            def _():
                x_copy(side, target).wait_send()
                x_arrival(side, target).wait_recv()
                for c in range(strips):
                    s[rb, c] = s[rb, c] + rx[side, c]

        lane_h = lax.broadcasted_iota(jnp.int32, (CH, half), 1)
        row_h = lax.broadcasted_iota(jnp.int32, (CH, half), 0)
        first_lane, last_lane = lane_h == 0, lane_h == half - 1

        def smooth_block(rb):
            for r in range(0, half, CH):
                lost = [None] * strips

                def lose(c, value):
                    lost[c] = value if lost[c] is None else lost[c] + value

                def weight(n, lo, hi):
                    return w[n, rb, r:r + CH, lo:hi]

                for part in range(2):
                    for j in range(ny):
                        lo = PAD + r + (half if part == 0 else 0)
                        left, right = j * half, j * half + full
                        x = b[rb + part, j, lo:lo + CH, :]
                        fore, aft = pltpu.roll(x, full - 1, 1), pltpu.roll(x, 1, 1)
                        new = (1.0 - relaxation) * x + weight(0, left, right) * b[rb + part, j, lo + 1:lo + 1 + CH, :]
                        new = new + weight(1, left, right) * b[rb + part, j, lo - 1:lo - 1 + CH, :]
                        new = new + weight(2, left, right) * jnp.where(not_last, fore, 0.0)
                        new = new + weight(3, left, right) * jnp.where(not_first, aft, 0.0)
                        mask = a[rb + part, j, lo:lo + CH, :] > 0
                        d[rb + part, j, lo:lo + CH, :] = jnp.where(mask, new, 0.0)
                        cut = jnp.where(mask, 0.0, new)
                        lose(j, cut[:, :half])
                        lose(j + 1, cut[:, half:])
                        if j + 2 < strips:
                            at = (j + 2) * half
                            lose(j + 2, weight(3, at, at + half) * jnp.where(first_lane, aft[:, :half], 0.0))
                        if j >= 1:
                            at = (j - 1) * half
                            lose(j - 1, weight(2, at, at + half) * jnp.where(last_lane, fore[:, half:], 0.0))
                for c in range(strips):
                    lk[rb, r:r + CH, c * half:(c + 1) * half] = lost[c]

        diagonal = lax.broadcasted_iota(jnp.int32, (half, half), 0) == lax.broadcasted_iota(jnp.int32, (half, half), 1)

        def record(rb, part):
            off = PAD + (half if part == 0 else 0)
            for side in range(2):
                at = side * half
                for j in range(ny):
                    x = b[rb + part, j, off:off + half, at:at + half]
                    inside = jnp.where(a[rb + part, j, PAD + half:PAD + half + PAD, at:at + half][0:1] > 0, 1.0, 0.0)
                    beyond = jnp.where(inside > 0, 0.0, pltpu.roll(inside, half - 1 if side == 0 else 1, 1))
                    edge_lane = pltpu.roll(beyond, 1 if side == 0 else half - 1, 1)
                    along = jnp.sum(x * edge_lane, axis=1, keepdims=True)
                    rim = x[:, 0:1] if side == 0 else x[:, half - 1:half]
                    q = off + half - 5 * PAD if part == 0 else off
                    near = b[rb + part, j, q:q + 5 * PAD, at:at + half]
                    here = a[rb + part, j, q:q + 5 * PAD, at:at + half]
                    step_ = 1 if part == 0 else -1
                    over = a[rb + part, j, q + step_:q + step_ + 5 * PAD, at:at + half]
                    count = jnp.sum(jnp.where(here > 0, 1.0, 0.0), axis=0, keepdims=True)
                    place = count + (half - 5 * PAD) if part == 0 else (5 * PAD - 1) - count
                    flat = jnp.sum(jnp.where(over > 0, 0.0, near), axis=0, keepdims=True)
                    rows = (jnp.sum(jnp.where(diagonal, along, 0.0), axis=0, keepdims=True), beyond, flat, place,
                            jnp.sum(jnp.where(diagonal, rim, 0.0), axis=0, keepdims=True))
                    for n, value in enumerate(rows):
                        rec[rb, side, part, j, n:n + 1, :] = value
                    rec[rb, side, part, j, len(rows):, :] = jnp.zeros((PAD - len(rows), half), jnp.float32)

        def past(value, part):
            return jnp.where(value[3:4] == (half if part == 0 else -1), value[2:3], 0.0)

        def e_send(rb):
            for side, has, target in z_sides:
                @pl.when(has)
                def _():
                    e_copy(side, target, rb).start()

        def e_wait(rb):
            for side, has, target in z_sides:
                @pl.when(has)
                def _():
                    e_arrival(side, target, rb).wait_recv()

        def c_send(side):
            _, has, target = x_sides[side]
            rb, part, before = (0, 1, 1) if side == 0 else (last, 0, last - 1)

            @pl.when(has)
            def _():
                for edge_side in range(2):
                    for j in range(ny):
                        rec[rb, edge_side, part, j, 5:6, :] = past(rec[before, edge_side, part, j], part)
                c_copy(side, target).start()

        def c_wait(side):
            _, has, target = x_sides[side]

            @pl.when(has)
            def _():
                c_copy(side, target).wait_send()
                c_arrival(side, target).wait_recv()

        def spread(value, r):
            here = lane_h == row_h + r
            return jnp.sum(jnp.where(here, value, 0.0), axis=1, keepdims=True)

        def lose_edge(rb, c, r, value, side, part):
            n = 2 if side == 0 else 3
            out = w[n, rb, r:r + CH, c * half:(c + 1) * half] * (spread(value[0:1], r) * value[1:2])
            if r == (half - CH if part == 0 else 0):
                line = jnp.where((row_h + r).astype(jnp.float32) == value[3:4], value[2:3], 0.0)
                out = out + w[1 - part, rb, r:r + CH, c * half:(c + 1) * half] * line
            return out

        def lose_rim(rb, c, r, values, side):
            lane = last_lane if side == 0 else first_lane
            total = spread(values, r)
            return w[2 if side == 0 else 3, rb, r:r + CH, c * half:(c + 1) * half] * jnp.where(lane, total, 0.0)

        def add_loss(rb, c, r, value):
            at = slice(c * half, (c + 1) * half)
            lk[rb, r:r + CH, at] = lk[rb, r:r + CH, at] + value

        def lose_rows(rb, part):
            for side in range(2):
                for j in range(ny):
                    value = rec[rb, side, part, j]
                    c = j + side
                    for r in range(0, half, CH):
                        add_loss(rb, c, r, lose_edge(rb, c, r, value, side, part))
                        other = c + (1 if side == 1 else -1)
                        if 0 <= other < strips:
                            add_loss(rb, other, r, lose_rim(rb, other, r, value[4:5], side))

        def passed(store, rb, part):
            if part == 0:
                return jnp.where(rb > 0, past(store(jnp.maximum(rb - 1, 0)), 0), store(rb)[5:6])
            return jnp.where(rb < nx, past(store(jnp.minimum(rb + 1, nx)), 1), store(rb)[5:6])

        def resolve(rb):
            @pl.when(rb == 0)
            def _():
                lose_rows(0, 0)

            @pl.when(rb == nx)
            def _():
                lose_rows(nx, 1)

            for c in range(strips):
                at = slice(c * half, (c + 1) * half)
                for r in range(0, half, CH):
                    lost = lk[rb, r:r + CH, at]
                    for side, own in ((1, 0), (0, strips - 1)):
                        z, k = (0, 1) if side == 1 else (1, 0)
                        if c == own:
                            for part in range(2):
                                lost = lost + lose_edge(rb, c, r, got[z, rb, part, k], side, part)
                            rim = got[z, rb, 0, 1 - k, 4:5] + got[z, rb, 1, 1 - k, 4:5]
                            lost = lost + lose_rim(rb, c, r, rim, side)
                        if c == own + (1 if side == 1 else -1):
                            rim = got[z, rb, 0, k, 4:5] + got[z, rb, 1, k, 4:5]
                            lost = lost + lose_rim(rb, c, r, rim, side)
                    for part, row in ((0, 0), (1, half - 1)):
                        if r <= row < r + CH:
                            over = None
                            for side, j in ((1, c - 1), (0, c)):
                                if 0 <= j < ny:
                                    term = passed(lambda k: rec[k, side, part, j], rb, part)
                                else:
                                    z, k_ = (0, 1) if side == 1 else (1, 0)
                                    term = passed(lambda k: got[z, k, part, k_], rb, part)
                                over = term if over is None else over + term
                            lost = lost + w[1 - part, rb, r:r + CH, at] * jnp.where(row_h + r == row, over, 0.0)
                    lk[rb, r:r + CH, at] = 1.0 / (1.0 - lost)

        def normalise(i, src, dst, scale):
            for j in range(ny):
                for r in range(0, full, CH):
                    rb = i + r // half
                    q = r % half
                    lo = PAD + r
                    value = src[i + 1, j, lo:lo + CH, :] * scale[rb, q:q + CH, j * half:j * half + full]
                    dst[i + 1, j, lo:lo + CH, :] = value

        lane = lax.broadcasted_iota(jnp.int32, (hw, half), 1)
        low_half = lane < hw
        lane8 = lax.broadcasted_iota(jnp.int32, (PAD, half), 1)

        def shifted_rows(lo, count):
            return pltpu.roll(px[pl.ds(lo, count), :], hw, 1)

        def pack(rb):
            lo = pl.multiple_of(rb * half + PAD, PAD)
            first = shifted_rows(lo, hw)
            second = shifted_rows(lo + hw, hw)
            m0, m1 = first[:, :half], second[:, :half]
            pk[1, rb, 0:hw, :] = jnp.where(low_half, m0, pltpu.roll(m1, hw, 1))
            pk[0, rb, 0:hw, :] = jnp.where(low_half, pltpu.roll(m0, hw, 1), m1)
            to_left = jnp.zeros((PAD, half), jnp.float32)
            to_right = to_left
            for k in range(half // PAD):
                part = first if k * PAD < hw else second
                q = k * PAD % hw
                e = part[q:q + PAD, half:]
                here = lane8 == k
                to_left = jnp.where(here, pltpu.roll(e, k, 1) if k else e, to_left)
                to_right = jnp.where(here, pltpu.roll(e, k + 1, 1), to_right)
            pk[0, rb, hw:hw + PAD, :] = to_left
            pk[1, rb, hw:hw + PAD, :] = to_right
            for side, has, target in z_sides:
                @pl.when(has)
                def _():
                    pk_copy(side, target, rb).start()

        def pack_ends():
            for n, lo in ((0, 0), (1, height - PAD)):
                hk[n] = shifted_rows(lo, PAD)[:, :half]
            for side, has, target in z_sides:
                @pl.when(has)
                def _():
                    hk_copy(side, target).start()

        def unpack(rb):
            for side, has, target in z_sides:
                @pl.when(has)
                def _():
                    pk_arrival(side, target, rb).wait_recv()
            lo = pl.multiple_of(rb * half + PAD, PAD)
            from_left, from_right = pr[0, rb, 0:hw, :], pr[1, rb, 0:hw, :]
            for n in range(2):
                start = lo + n * hw
                rolled = shifted_rows(start, hw)
                m = rolled[:, :half]
                fl = pltpu.roll(from_left, hw, 1) if n else from_left
                fr = from_right if n else pltpu.roll(from_right, hw, 1)
                pe[pl.ds(start, hw), half:2 * half] = jnp.where(low_half, fl, m)
                pe[pl.ds(start, hw), 2 * half:3 * half] = rolled[:, half:]
                pe[pl.ds(start, hw), 3 * half:4 * half] = jnp.where(low_half, m, fr)
            cl, cr = pr[0, rb, hw:hw + PAD, :], pr[1, rb, hw:hw + PAD, :]
            for k in range(half // PAD):
                pe[pl.ds(lo + k * PAD, PAD), 0:half] = pltpu.roll(cl, half - 1 - k, 1)
                pe[pl.ds(lo + k * PAD, PAD), 4 * half:5 * half] = pltpu.roll(cr, half - k, 1) if k else cr

        def unpack_ends():
            for side, has, target in z_sides:
                @pl.when(has)
                def _():
                    hk_arrival(side, target).wait_recv()
            low8 = lane8 < hw
            for n, lo in ((0, 0), (1, height - PAD)):
                rolled = shifted_rows(lo, PAD)
                m = rolled[:, :half]
                pe[lo:lo + PAD, half:2 * half] = jnp.where(low8, hr[0, n], m)
                pe[lo:lo + PAD, 2 * half:3 * half] = rolled[:, half:]
                pe[lo:lo + PAD, 3 * half:4 * half] = jnp.where(low8, m, hr[1, n])

        wide = (strips + 2) * half
        step = 2 * PAD

        def weigh(rb):
            @pl.loop(0, half // step, unroll=8)
            def _(c):
                q = pl.multiple_of(c * step, step)
                lo = pl.multiple_of(rb * half + PAD + q, PAD)
                block = pe[pl.ds(lo - PAD, step + 2 * PAD), half:wide - half]
                line = pe[pl.ds(lo, step), :]
                mid = block[PAD:PAD + step]
                east = block[PAD + 1:PAD + 1 + step]
                west = block[PAD - 1:PAD - 1 + step]
                north = pltpu.roll(line, wide - 1, 1)[:, half:wide - half]
                south = pltpu.roll(line, 1, 1)[:, half:wide - half]
                se, sw, sn, ss = mid + east, mid + west, mid + north, mid + south
                across, along = sn * ss, se * sw
                ne, nw = east * sw * across, west * se * across
                nn, ns = north * ss * along, south * sn * along
                scale = relaxation / jnp.maximum((ne + nw) + (nn + ns), 1e-30)
                for n, face in enumerate((ne, nw, nn, ns)):
                    w[n, rb, pl.ds(q, step), :] = face * scale

        peers = sum(jnp.where(has, 1, 0) for _, has, _t in z_sides + x_sides)
        pl.semaphore_wait(barrier, peers)

        for side, has, target in x_sides:
            @pl.when(has)
            def _():
                row_copy(side, target).start()
        own.wait()

        @pl.loop(1, nx)
        def _(rb):
            pack(rb)

        for side, has, target in x_sides:
            @pl.when(has)
            def _():
                row_arrival(side, target).wait_recv()

        @pl.loop(0, 2)
        def _(n):
            pack(n * nx)

        pack_ends()

        @pl.loop(1, 4)
        def _(rb):
            unpack(rb)

        weigh(need_1[0][0])

        def finish(k, i):
            rb = pick(k, ready_1)

            @pl.when(rb >= 0)
            def _():
                partial(rb)
                z_send(rb)

            @pl.when(k >= nx - 2)
            def _():
                partial(jnp.where(i == 0, 0, nx))

            @pl.when(k == nx - 2)
            def _():
                x_send(0)

            @pl.when(k == nx - 1)
            def _():
                x_send(1)

        next_pe = [4 + k for k in range(nx - 4)] + [0, nx, -1, -1]

        @pl.loop(0, nx)
        def _(k):
            i = pick(k, rows_1)
            a_copy(i).wait()
            nxt = pick(k, next_pe)

            @pl.when(nxt >= 0)
            def _():
                unpack(nxt)

            @pl.when(k == nx - 2)
            def _():
                unpack_ends()

            weigh(pick(k, [n[-1] for n in need_1]))
            smooth_row(i)
            finish(k, i)

        x_add(0)
        z_send(0)
        x_add(1)
        z_send(last)

        invert(need_2[0][0])

        def edges(rb):
            smooth_block(rb)
            record(rb, 0)
            record(rb, 1)
            e_send(rb)

        @pl.loop(0, nx)
        def _(k):
            i = pick(k, rows_2)
            invert(pick(k, [n[-1] for n in need_2]))
            normalise(i, b, b, inv)
            rb = pick(k, ready_2)

            @pl.when(rb >= 0)
            def _():
                edges(rb)

            @pl.when(k == nx - 2)
            def _():
                smooth_block(0)
                record(0, 1)
                c_send(0)

            @pl.when(k == nx - 1)
            def _():
                smooth_block(nx)
                record(nx, 0)
                c_send(1)

        c_wait(0)
        e_send(0)
        c_wait(1)
        e_send(last)

        seen_e, wait_e = set(), []
        for n in [need_2[0][:1]] + [[need_2[0][-1]]] + need_2[1:]:
            new = [q for q in (n[-1] - 1, n[-1], n[-1] + 1) if 0 <= q <= nx and q not in seen_e]
            seen_e.update(new)
            wait_e.append(new)
        for rb in wait_e[0]:
            e_wait(rb)
        resolve(need_2[0][0])
        width = max(len(n) for n in wait_e[1:])

        @pl.loop(0, nx)
        def _(k):
            i = pick(k, rows_2)
            for q in range(width):
                rb = pick(k, [n[q] if q < len(n) else -1 for n in wait_e[1:]])

                @pl.when(rb >= 0)
                def _():
                    e_wait(rb)

            resolve(pick(k, [need_2[0][-1]] + [n[-1] for n in need_2[1:]]))
            normalise(i, d, a, lk)
            o_copy(i).start()

        @pl.loop(0, nx)
        def _(i):
            o_copy(i).wait()

        for side, has, target in z_sides:
            @pl.when(has)
            def _():
                @pl.loop(0, nx + 1)
                def _(rb):
                    z_copy(side, target, rb).wait_send()
                    e_copy(side, target, rb).wait_send()
                    pk_copy(side, target, rb).wait_send()
                hk_copy(side, target).wait_send()

        for side, has, target in x_sides:
            @pl.when(has)
            def _():
                row_copy(side, target).wait_send()

    return kernel


def local(permeability, basis, support):
    nx, ny, full, _ = basis.shape
    half = full // 2
    size_x, size_y = lax.axis_size("gx"), lax.axis_size("gy")
    height = permeability.shape[0] + half + 2 * PAD
    f32 = jnp.float32
    strips = ny + 1
    scratch = [
        pltpu.VMEM((nx + 2, ny, full + 2 * PAD, full), f32),
        pltpu.VMEM((nx + 2, ny, full + 2 * PAD, full), f32),
        pltpu.VMEM((nx + 2, ny, full + 2 * PAD, full), f32),
        pltpu.VMEM((4, nx + 1, half, strips * half), f32),
        pltpu.VMEM((nx + 1, strips, half, half), f32),
        pltpu.VMEM((nx + 1, half, strips * half), f32),
        pltpu.VMEM((nx + 1, half, strips * half), f32),
        pltpu.VMEM((2, nx + 1, half, half), f32),
        pltpu.VMEM((2, strips, half, half), f32),
        pltpu.VMEM((nx + 1, 2, 2, ny, PAD, half), f32),
        pltpu.VMEM((2, nx + 1, 2, 2, PAD, half), f32),
        pltpu.VMEM((height, full), f32),
        pltpu.VMEM((height, (strips + 2) * half), f32),
        pltpu.VMEM((2, nx + 1, half // 2 + PAD, half), f32),
        pltpu.VMEM((2, nx + 1, half // 2 + PAD, half), f32),
        pltpu.VMEM((2, PAD, half), f32),
        pltpu.VMEM((2, 2, PAD, half), f32),
        pltpu.SemaphoreType.DMA((nx,)),
        pltpu.SemaphoreType.DMA,
        pltpu.SemaphoreType.DMA((nx,)),
        pltpu.SemaphoreType.DMA((ITERS, 2, nx + 1)),
        pltpu.SemaphoreType.DMA((ITERS, 2, nx + 1)),
        pltpu.SemaphoreType.DMA((ITERS, 2)),
        pltpu.SemaphoreType.DMA((ITERS, 2)),
        pltpu.SemaphoreType.DMA((2, nx + 1)),
        pltpu.SemaphoreType.DMA((2, nx + 1)),
        pltpu.SemaphoreType.DMA((2,)),
        pltpu.SemaphoreType.DMA((2,)),
        pltpu.SemaphoreType.DMA((2,)),
        pltpu.SemaphoreType.DMA((2,)),
    ]
    return pl.pallas_call(
        make_kernel(nx, ny, size_x, size_y, half),
        out_shape=jax.ShapeDtypeStruct(basis.shape, f32),
        in_specs=[pl.BlockSpec(memory_space=pltpu.HBM)] * 2,
        out_specs=pl.BlockSpec(memory_space=pl.ANY),
        scratch_shapes=scratch,
        compiler_params=pltpu.CompilerParams(
            collective_id=0, has_side_effects=True, vmem_limit_bytes=48 * 1024 * 1024),
        name="smoothing",
    )(*[pltpu.with_memory_space_constraint(x, pltpu.HBM) for x in (permeability, basis)])


def solution(mesh):
    placed = (P("gx", "gy"), P("gx", "gy", None, None), P("gx", "gy", None, None))
    return jax.shard_map(
        local, mesh=mesh, in_specs=placed, out_specs=P("gx", "gy", None, None), check_vma=False
    )
```

```python
import jax
import jax.numpy as jnp
from jax import lax
from jax.experimental import pallas as pl
from jax.experimental.pallas import tpu as pltpu
from jax.sharding import PartitionSpec as P

MESH = pl.DeviceIdType.MESH
relaxation = 2.0 / 3.0
coupling = relaxation / (1.0 - relaxation)
PAD = 8
CH = 16
NEAR = 40


def pick(k, table):
    value = jnp.int32(table[-1])
    for n in range(len(table) - 2, -1, -1):
        value = jnp.where(k == n, table[n], value)
    return value


def first_needs(order, count):
    seen, out = set(), []
    for rb in order:
        new = [q for q in (rb - 1, rb, rb + 1) if 0 <= q < count and q not in seen]
        seen.update(new)
        out.append(new)
    return out


def make_kernel(nx, ny, size_x, size_y, half):
    full = 2 * half
    last = nx
    strips = ny + 1
    hw = half // 2

    middle = list(range(3, nx - 2))
    pack_order = [1, nx - 1, 2, 0, nx, nx - 2] + middle
    weigh_order = [0, 1, nx, nx - 1, 2] + middle + [nx - 2]
    unpack_steps = first_needs(weigh_order, nx + 1)
    total_order = [1, nx - 1, 2, 3, 0, nx] + middle[1:] + [nx - 2]
    assert sorted(weigh_order) == sorted(pack_order) == sorted(total_order) == list(range(nx + 1))
    events, done, known = [], set(), set()
    for rb in total_order + [-1] * (nx + 1):
        known.add(rb)
        ready = [q for q in range(nx + 1) if q not in done and all(n in known for n in (q - 1, q, q + 1) if 0 <= n <= nx)]
        done.update(ready[:1])
        if rb >= 0 or ready:
            events.append((rb, ready[0] if ready else -1))
    assert len(done) == nx + 1
    resolve_order = [2, 3, 1, 0, nx] + [q for q in range(4, nx)]
    assert sorted(resolve_order) == list(range(nx + 1))
    resolve_steps = first_needs(resolve_order, nx + 1)

    def kernel(*refs):
        (perm_h, basis_h, out_h,
         a, b, d, w, s, lk, rz, rx, rec, got, px, pe, pk, pr, hk, hr,
         a_sem, p_sem, o_sem, zs_sem, zr_sem, xs_sem, xr_sem,
         ps_sem, pr_sem, hs_sem, hr_sem, rs_sem, rr_sem) = refs
        gx, gy = lax.axis_index("gx"), lax.axis_index("gy")
        has_up, has_down = gx > 0, gx < size_x - 1
        has_left, has_right = gy > 0, gy < size_y - 1
        up, down = (gx - 1, gy), (gx + 1, gy)
        left, right = (gx, gy - 1), (gx, gy + 1)
        z_sides = ((0, has_left, left), (1, has_right, right))
        x_sides = ((0, has_up, up), (1, has_down, down))
        halo = hw + PAD
        height = px.shape[0]
        length = height - 2 * halo

        def remote(src, dst, send, recv, target):
            return pltpu.make_async_remote_copy(
                src_ref=src, dst_ref=dst, send_sem=send, recv_sem=recv, device_id=target, device_id_type=MESH)

        def a_copy(i, h):
            return pltpu.make_async_copy(
                basis_h.at[i, :, :, pl.ds(h * half, half)], a.at[i + 1, :, h, pl.ds(PAD, full), :], a_sem.at[i, h])

        def o_copy(rb, part, h):
            lo = half if part == 0 else 0
            return pltpu.make_async_copy(
                d.at[rb + part, :, h, pl.ds(PAD + lo, half), :],
                out_h.at[rb - 1 + part, :, pl.ds(lo, half), pl.ds(h * half, half)], o_sem.at[rb, part, h])

        def row_copy(side, target):
            src, dst = (0, height - halo) if side == 0 else (length - halo, 0)
            return remote(perm_h.at[pl.ds(src, halo), :], px.at[pl.ds(dst, halo), :],
                          rs_sem.at[side], rr_sem.at[1 - side], target)

        def row_arrival(side, target):
            dst = 0 if side == 0 else height - halo
            return remote(perm_h.at[pl.ds(0, halo), :], px.at[pl.ds(dst, halo), :],
                          rs_sem.at[side], rr_sem.at[side], target)

        def pk_copy(side, target, rb):
            return remote(pk.at[side, rb], pr.at[1 - side, rb], ps_sem.at[side, rb], pr_sem.at[1 - side, rb], target)

        def pk_arrival(side, target, rb):
            return remote(pk.at[side, rb], pr.at[side, rb], ps_sem.at[side, rb], pr_sem.at[side, rb], target)

        def hk_copy(side, target):
            return remote(hk, hr.at[1 - side], hs_sem.at[side], hr_sem.at[1 - side], target)

        def hk_arrival(side, target):
            return remote(hk, hr.at[side], hs_sem.at[side], hr_sem.at[side], target)

        def z_copy(side, target, rb):
            strip = 0 if side == 0 else strips - 1
            return remote(s.at[rb, strip], rz.at[1 - side, rb], zs_sem.at[0, side, rb], zr_sem.at[0, 1 - side, rb], target)

        def z_arrival(side, target, rb):
            return remote(s.at[rb, 0], rz.at[side, rb], zs_sem.at[0, side, rb], zr_sem.at[0, side, rb], target)

        def x_copy(side, target):
            rb = 0 if side == 0 else last
            return remote(s.at[rb], rx.at[1 - side], xs_sem.at[0, side], xr_sem.at[0, 1 - side], target)

        def x_arrival(side, target):
            return remote(s.at[0], rx.at[side], xs_sem.at[0, side], xr_sem.at[0, side], target)

        def pair(rb, side):
            return rec.at[rb, side, :, pl.ds(0 if side == 0 else ny - 2, 2)]

        def e_copy(side, target, rb):
            return remote(pair(rb, side), got.at[1 - side, rb], zs_sem.at[1, side, rb], zr_sem.at[1, 1 - side, rb], target)

        def e_arrival(side, target, rb):
            return remote(pair(rb, side), got.at[side, rb], zs_sem.at[1, side, rb], zr_sem.at[1, side, rb], target)

        def c_copy(side, target):
            src, dst, part = (0, last, 1) if side == 0 else (last, 0, 0)
            return remote(rec.at[src, :, part], rec.at[dst, :, part], xs_sem.at[1, side], xr_sem.at[1, 1 - side], target)

        def c_arrival(side, target):
            rb, part = (0, 0) if side == 0 else (last, 1)
            return remote(rec.at[rb, :, part], rec.at[rb, :, part], xs_sem.at[1, side], xr_sem.at[1, side], target)

        def each(sides, act):
            for side, has, target in sides:
                @pl.when(has)
                def _():
                    act(side, target)

        barrier = pltpu.get_barrier_semaphore()
        each(z_sides + x_sides, lambda side, target: pl.semaphore_signal(
            barrier, inc=1, device_id=target, device_id_type=MESH))

        own = pltpu.make_async_copy(perm_h, px.at[pl.ds(halo, length), :], p_sem)
        own.start()

        @pl.loop(0, nx)
        def _(k):
            i = pick(k, [0, nx - 1, 1, nx - 2] + list(range(2, nx - 2)))
            a_copy(i, 0).start()
            a_copy(i, 1).start()

        edge = jnp.zeros((PAD, half), jnp.float32)

        @pl.loop(0, nx)
        def _(i):
            for buf in (a, b):
                for j in range(ny):
                    for h in range(2):
                        buf[i + 1, j, h, 0:PAD, :] = edge
                        buf[i + 1, j, h, PAD + full:, :] = edge

        for buf in (a, b):
            for j in range(ny):
                for h in range(2):
                    buf[0, j, h, half:, :] = jnp.zeros((2 * PAD + half, half), jnp.float32)
                    buf[nx + 1, j, h, 0:2 * PAD + half, :] = jnp.zeros((2 * PAD + half, half), jnp.float32)

        for side, has, _t in z_sides:
            @pl.when(jnp.logical_not(has))
            def _():
                @pl.loop(0, nx + 1)
                def _(rb):
                    rz[side, rb] = jnp.zeros((half, half), jnp.float32)
                    got[side, rb] = jnp.zeros((2, 2, PAD, half), jnp.float32)
                    pr[side, rb] = jnp.zeros((hw + PAD, half), jnp.float32)
                hr[side] = jnp.zeros((2, PAD, half), jnp.float32)

        for side, has, _t in x_sides:
            @pl.when(jnp.logical_not(has))
            def _():
                lo = 0 if side == 0 else height - halo
                px[lo:lo + halo, :] = jnp.zeros((halo, full), jnp.float32)
                rb, part = (0, 0) if side == 0 else (last, 1)
                rec[rb, :, part] = jnp.zeros((2, ny, PAD, half), jnp.float32)

        lane = lax.broadcasted_iota(jnp.int32, (hw, half), 1)
        low_half = lane < hw
        lane8 = lax.broadcasted_iota(jnp.int32, (PAD, half), 1)

        def shifted_rows(lo, count):
            return pltpu.roll(px[pl.ds(lo, count), :], hw, 1)

        def pack(rb):
            lo = pl.multiple_of(rb * half + PAD, PAD)
            first = shifted_rows(lo, hw)
            second = shifted_rows(lo + hw, hw)
            m0, m1 = first[:, :half], second[:, :half]
            for n, part in ((0, first), (1, second)):
                pe[1, pl.ds(lo + n * hw, hw), :] = part[:, :half]
                pe[2, pl.ds(lo + n * hw, hw), :] = part[:, half:]
            pk[1, rb, 0:hw, :] = jnp.where(low_half, m0, pltpu.roll(m1, hw, 1))
            pk[0, rb, 0:hw, :] = jnp.where(low_half, pltpu.roll(m0, hw, 1), m1)
            to_left = jnp.zeros((PAD, half), jnp.float32)
            to_right = to_left
            for k in range(half // PAD):
                part = first if k * PAD < hw else second
                q = k * PAD % hw
                e = part[q:q + PAD, half:]
                here = lane8 == k
                to_left = jnp.where(here, pltpu.roll(e, k, 1) if k else e, to_left)
                to_right = jnp.where(here, pltpu.roll(e, k + 1, 1), to_right)
            pk[0, rb, hw:hw + PAD, :] = to_left
            pk[1, rb, hw:hw + PAD, :] = to_right
            each(z_sides, lambda side, target: pk_copy(side, target, rb).start())

        ends = ((0, 0), (1, height - PAD))

        def pack_ends():
            for n, lo in ends:
                rolled = shifted_rows(lo, PAD)
                hk[n] = rolled[:, :half]
                pe[2, lo:lo + PAD, :] = rolled[:, half:]
            each(z_sides, lambda side, target: hk_copy(side, target).start())

        def unpack(rb):
            each(z_sides, lambda side, target: pk_arrival(side, target, rb).wait_recv())
            lo = pl.multiple_of(rb * half + PAD, PAD)
            from_left, from_right = pr[0, rb, 0:hw, :], pr[1, rb, 0:hw, :]
            for n in range(2):
                start = lo + n * hw
                m = pe[1, pl.ds(start, hw), :]
                fl = pltpu.roll(from_left, hw, 1) if n else from_left
                fr = from_right if n else pltpu.roll(from_right, hw, 1)
                pe[1, pl.ds(start, hw), :] = jnp.where(low_half, fl, m)
                pe[3, pl.ds(start, hw), :] = jnp.where(low_half, m, fr)
            cl, cr = pr[0, rb, hw:hw + PAD, :], pr[1, rb, hw:hw + PAD, :]
            for k in range(half // PAD):
                pe[0, pl.ds(lo + k * PAD, PAD), :] = pltpu.roll(cl, half - 1 - k, 1)
                pe[4, pl.ds(lo + k * PAD, PAD), :] = pltpu.roll(cr, half - k, 1) if k else cr

        def unpack_ends():
            each(z_sides, lambda side, target: hk_arrival(side, target).wait_recv())
            low8 = lane8 < hw
            for n, lo in ends:
                pe[1, lo:lo + PAD, :] = jnp.where(low8, hr[0, n], hk[n])
                pe[3, lo:lo + PAD, :] = jnp.where(low8, hk[n], hr[1, n])

        lane_h = lax.broadcasted_iota(jnp.int32, (CH, half), 1)
        row_h = lax.broadcasted_iota(jnp.int32, (CH, half), 0)
        first_lane, last_lane = lane_h == 0, lane_h == half - 1

        def ahead(x):
            return pltpu.roll(x, half - 1, 1)

        def behind(x):
            return pltpu.roll(x, 1, 1)

        def weigh(rb):
            base = pl.multiple_of(rb * half + PAD, PAD)
            for r in range(0, half, CH):
                mids = [pe[c, pl.ds(base + r, CH), :] for c in range(strips + 2)]
                fores = [ahead(x) if c else None for c, x in enumerate(mids)]
                afts = [behind(x) if c < strips + 1 else None for c, x in enumerate(mids)]
                for c in range(1, strips + 1):
                    mid = mids[c]
                    east = pe[c, pl.ds(base + r + 1, CH), :]
                    west = pe[c, pl.ds(base + r - 1, CH), :]
                    north = jnp.where(last_lane, fores[c + 1], fores[c])
                    south = jnp.where(first_lane, afts[c - 1], afts[c])
                    se, sw, sn, ss = mid + east, mid + west, mid + north, mid + south
                    across, along = sn * ss, se * sw
                    ne, nw = east * sw * across, west * se * across
                    nn, ns = north * ss * along, south * sn * along
                    scale = coupling / jnp.maximum((ne + nw) + (nn + ns), 1e-30)
                    for n, face in enumerate((ne, nw, nn, ns)):
                        w[n, rb, c - 1, r:r + CH, :] = face * scale

        def accumulate(store, c, value):
            store[c] = value if store[c] is None else store[c] + value

        def update(src, rb, r, part, j):
            lo = PAD + r + (half if part == 0 else 0)
            xs = [src[rb + part, j, h, lo:lo + CH, :] for h in range(2)]
            fores, afts = [ahead(x) for x in xs], [behind(x) for x in xs]
            fore = (jnp.where(last_lane, fores[1], fores[0]), jnp.where(last_lane, 0.0, fores[1]))
            aft = (jnp.where(first_lane, 0.0, afts[0]), jnp.where(first_lane, afts[0], afts[1]))
            news = []
            for h in range(2):
                c = j + h
                new = xs[h] + w[0, rb, c, r:r + CH, :] * src[rb + part, j, h, lo + 1:lo + 1 + CH, :]
                new = new + w[1, rb, c, r:r + CH, :] * src[rb + part, j, h, lo - 1:lo - 1 + CH, :]
                new = new + w[2, rb, c, r:r + CH, :] * fore[h]
                news.append(new + w[3, rb, c, r:r + CH, :] * aft[h])
            return lo, xs, news, fores[1], afts[1], fores[0], afts

        def smooth_first(rb):
            for r in range(0, half, CH):
                total = [None] * strips
                for part in range(2):
                    for j in range(ny):
                        lo, xs, news, *_ = update(a, rb, r, part, j)
                        for h in range(2):
                            value = jnp.where(xs[h] > 0, news[h], 0.0)
                            b[rb + part, j, h, lo:lo + CH, :] = value
                            accumulate(total, j + h, value)
                for c in range(strips):
                    s[rb, c, r:r + CH, :] = total[c]

        def smooth_second(rb):
            for r in range(0, half, CH):
                lost = [None] * strips
                for part in range(2):
                    for j in range(ny):
                        lo, xs, news, _, aft_end, fore_start, _a = update(b, rb, r, part, j)
                        for h in range(2):
                            mask = a[rb + part, j, h, lo:lo + CH, :] > 0
                            d[rb + part, j, h, lo:lo + CH, :] = jnp.where(mask, news[h], 0.0)
                            accumulate(lost, j + h, jnp.where(mask, 0.0, news[h]))
                        if j + 2 < strips:
                            accumulate(lost, j + 2, w[3, rb, j + 2, r:r + CH, :] * jnp.where(first_lane, aft_end, 0.0))
                        if j >= 1:
                            accumulate(lost, j - 1, w[2, rb, j - 1, r:r + CH, :] * jnp.where(last_lane, fore_start, 0.0))
                for c in range(strips):
                    lk[rb, c, r:r + CH, :] = lost[c]

        def normalise(rb):
            each(z_sides, lambda side, target: z_arrival(side, target, rb).wait_recv())
            for c in range(strips):
                for r in range(0, half, CH):
                    total = s[rb, c, r:r + CH, :]
                    if c == 0:
                        total = total + rz[0, rb, r:r + CH, :]
                    if c == strips - 1:
                        total = total + rz[1, rb, r:r + CH, :]
                    scale = 1.0 / jnp.where(total > 0, total, 1.0)
                    for j, h in ((c - 1, 1), (c, 0)):
                        if 0 <= j < ny:
                            for part in range(2):
                                lo = PAD + r + (half if part == 0 else 0)
                                b[rb + part, j, h, lo:lo + CH, :] = b[rb + part, j, h, lo:lo + CH, :] * scale

        diagonal = lax.broadcasted_iota(jnp.int32, (half, half), 0) == lax.broadcasted_iota(jnp.int32, (half, half), 1)

        def record(rb, part):
            off = PAD + (half if part == 0 else 0)
            for side in range(2):
                for j in range(ny):
                    x = b[rb + part, j, side, off:off + half, :]
                    inside = jnp.where(a[rb + part, j, side, PAD + half:PAD + half + 1, :] > 0, 1.0, 0.0)
                    beyond = jnp.where(inside > 0, 0.0, ahead(inside) if side == 0 else behind(inside))
                    edge_lane = behind(beyond) if side == 0 else ahead(beyond)
                    along = jnp.sum(x * edge_lane, axis=1, keepdims=True)
                    rim = x[:, 0:1] if side == 0 else x[:, half - 1:half]
                    q = off + half - NEAR if part == 0 else off
                    beside = 1 if part == 0 else -1
                    near = b[rb + part, j, side, q:q + NEAR, :]
                    here = a[rb + part, j, side, q:q + NEAR, :]
                    over = a[rb + part, j, side, q + beside:q + beside + NEAR, :]
                    count = jnp.sum(jnp.where(here > 0, 1.0, 0.0), axis=0, keepdims=True)
                    place = count + (half - NEAR) if part == 0 else (NEAR - 1) - count
                    flat = jnp.sum(jnp.where(over > 0, 0.0, near), axis=0, keepdims=True)
                    rows = (jnp.sum(jnp.where(diagonal, along, 0.0), axis=0, keepdims=True), beyond, flat, place,
                            jnp.sum(jnp.where(diagonal, rim, 0.0), axis=0, keepdims=True))
                    for n, value in enumerate(rows):
                        rec[rb, side, part, j, n:n + 1, :] = value
                    rec[rb, side, part, j, len(rows):, :] = jnp.zeros((PAD - len(rows), half), jnp.float32)

        def past(value, part):
            return jnp.where(value[3:4] == (half if part == 0 else -1), value[2:3], 0.0)

        def e_send(rb):
            each(z_sides, lambda side, target: e_copy(side, target, rb).start())

        def c_send(side):
            _, has, target = x_sides[side]
            rb, part, before = (0, 1, 1) if side == 0 else (last, 0, last - 1)

            @pl.when(has)
            def _():
                for edge_side in range(2):
                    for j in range(ny):
                        rec[rb, edge_side, part, j, 5:6, :] = past(rec[before, edge_side, part, j], part)
                c_copy(side, target).start()

        def spread(value, r):
            return jnp.sum(jnp.where(lane_h == row_h + r, value, 0.0), axis=1, keepdims=True)

        def lose_edge(rb, c, r, value, side, part):
            out = w[2 if side == 0 else 3, rb, c, r:r + CH, :] * (spread(value[0:1], r) * value[1:2])
            if (r + CH > half - NEAR) if part == 0 else (r < NEAR):
                line = jnp.where((row_h + r).astype(jnp.float32) == value[3:4], value[2:3], 0.0)
                out = out + w[1 - part, rb, c, r:r + CH, :] * line
            return out

        def lose_rim(rb, c, r, values, side):
            rim_lane = last_lane if side == 0 else first_lane
            return w[2 if side == 0 else 3, rb, c, r:r + CH, :] * jnp.where(rim_lane, spread(values, r), 0.0)

        def lose_rows(rb, part):
            for side in range(2):
                for j in range(ny):
                    value = rec[rb, side, part, j]
                    c = j + side
                    other = c + (1 if side == 1 else -1)
                    for r in range(0, half, CH):
                        lk[rb, c, r:r + CH, :] = lk[rb, c, r:r + CH, :] + lose_edge(rb, c, r, value, side, part)
                        if 0 <= other < strips:
                            lk[rb, other, r:r + CH, :] = lk[rb, other, r:r + CH, :] + lose_rim(rb, other, r, value[4:5], side)

        def passed(store, rb, part):
            if part == 0:
                return jnp.where(rb > 0, past(store(jnp.maximum(rb - 1, 0)), 0), store(rb)[5:6])
            return jnp.where(rb < nx, past(store(jnp.minimum(rb + 1, nx)), 1), store(rb)[5:6])

        def resolve(rb):
            @pl.when(rb == 0)
            def _():
                lose_rows(0, 0)

            @pl.when(rb == nx)
            def _():
                lose_rows(nx, 1)

            for c in range(strips):
                for r in range(0, half, CH):
                    lost = lk[rb, c, r:r + CH, :]
                    for z, k, side, own in ((0, 1, 1, 0), (1, 0, 0, strips - 1)):
                        if c == own:
                            for part in range(2):
                                lost = lost + lose_edge(rb, c, r, got[z, rb, part, k], side, part)
                            rim = got[z, rb, 0, 1 - k, 4:5, :] + got[z, rb, 1, 1 - k, 4:5, :]
                            lost = lost + lose_rim(rb, c, r, rim, side)
                        if c == own + (1 if side == 1 else -1):
                            rim = got[z, rb, 0, k, 4:5, :] + got[z, rb, 1, k, 4:5, :]
                            lost = lost + lose_rim(rb, c, r, rim, side)
                    for part, row in ((0, 0), (1, half - 1)):
                        if r <= row < r + CH:
                            over = [None]
                            for side, j, z, k in ((1, c - 1, 0, 1), (0, c, 1, 0)):
                                if 0 <= j < ny:
                                    accumulate(over, 0, passed(lambda q: rec[q, side, part, j], rb, part))
                                else:
                                    accumulate(over, 0, passed(lambda q: got[z, q, part, k], rb, part))
                            lost = lost + w[1 - part, rb, c, r:r + CH, :] * jnp.where(row_h + r == row, over[0], 0.0)
                    scale = 1.0 / ((1.0 + coupling) - lost)
                    for j, h in ((c - 1, 1), (c, 0)):
                        if 0 <= j < ny:
                            for part in range(2):
                                lo = PAD + r + (half if part == 0 else 0)
                                d[rb + part, j, h, lo:lo + CH, :] = d[rb + part, j, h, lo:lo + CH, :] * scale

        def o_each(rb, act):
            for part, inside in ((0, rb > 0), (1, rb < nx)):
                @pl.when(inside)
                def _():
                    for h in range(2):
                        act(o_copy(rb, part, h))

        peers = sum(jnp.where(has, 1, 0) for _, has, _t in z_sides + x_sides)
        pl.semaphore_wait(barrier, peers)

        each(x_sides, lambda side, target: row_copy(side, target).start())
        own.wait()

        @pl.loop(0, nx + 1)
        def _(k):
            rb = pick(k, pack_order)

            @pl.when(rb == 0)
            def _():
                each(x_sides, lambda side, target: row_arrival(side, target).wait_recv())
                pack_ends()

            pack(rb)

        @pl.loop(0, nx)
        def _(i):
            a_copy(i, 0).wait()
            a_copy(i, 1).wait()

        for n, rb in enumerate(unpack_steps[0]):
            unpack(rb)
        unpack_ends()
        width = max(len(n) for n in unpack_steps[1:])

        @pl.loop(0, nx + 1)
        def _(k):
            rb = pick(k, weigh_order)
            for q in range(width):
                new = pick(k, [-1] + [n[q] if q < len(n) else -1 for n in unpack_steps[1:]])

                @pl.when(new >= 0)
                def _():
                    unpack(new)

            weigh(rb)
            smooth_first(rb)

            for side, at in ((0, 0), (1, nx)):
                @pl.when(rb == at)
                def _():
                    _, has, target = x_sides[side]

                    @pl.when(has)
                    def _():
                        x_copy(side, target).start()

            @pl.when(jnp.logical_and(rb > 0, rb < nx))
            def _():
                each(z_sides, lambda side, target: z_copy(side, target, rb).start())

            @pl.when(rb == 3)
            def _():
                for side, at in ((0, 0), (1, nx)):
                    _, has, target = x_sides[side]

                    @pl.when(has)
                    def _():
                        x_copy(side, target).wait_send()
                        x_arrival(side, target).wait_recv()
                        for c in range(strips):
                            s[at, c] = s[at, c] + rx[side, c]
                    each(z_sides, lambda z, to: z_copy(z, to, at).start())

        @pl.loop(0, len(events))
        def _(k):
            rb = pick(k, [n for n, _ in events])

            @pl.when(rb >= 0)
            def _():
                normalise(rb)

                @pl.when(rb > 0)
                def _():
                    record(rb, 0)

                @pl.when(rb < nx)
                def _():
                    record(rb, 1)

                for side, at in ((0, 0), (1, nx)):
                    @pl.when(rb == at)
                    def _():
                        c_send(side)

                @pl.when(jnp.logical_and(rb > 0, rb < nx))
                def _():
                    e_send(rb)

            again = pick(k, [n for _, n in events])

            @pl.when(again >= 0)
            def _():
                smooth_second(again)

            @pl.when(k == nx - 1)
            def _():
                def arrive(side, target):
                    c_copy(side, target).wait_send()
                    c_arrival(side, target).wait_recv()
                each(x_sides, arrive)
                e_send(0)
                e_send(nx)

        width = max(len(n) for n in resolve_steps)

        @pl.loop(0, nx + 1)
        def _(k):
            for q in range(width):
                new = pick(k, [n[q] if q < len(n) else -1 for n in resolve_steps])

                @pl.when(new >= 0)
                def _():
                    each(z_sides, lambda side, target: e_arrival(side, target, new).wait_recv())

            rb = pick(k, resolve_order)
            resolve(rb)
            o_each(rb, lambda copy: copy.start())

        @pl.loop(0, nx + 1)
        def _(rb):
            o_each(rb, lambda copy: copy.wait())

        def drain(side, target):
            @pl.loop(0, nx + 1)
            def _(rb):
                z_copy(side, target, rb).wait_send()
                e_copy(side, target, rb).wait_send()
                pk_copy(side, target, rb).wait_send()
            hk_copy(side, target).wait_send()
        each(z_sides, drain)
        each(x_sides, lambda side, target: row_copy(side, target).wait_send())

    return kernel


def local(permeability, basis, support):
    nx, ny, full, _ = basis.shape
    half = full // 2
    size_x, size_y = lax.axis_size("gx"), lax.axis_size("gy")
    height = permeability.shape[0] + half + 2 * PAD
    f32 = jnp.float32
    strips = ny + 1
    boxes = pltpu.VMEM((nx + 2, ny, 2, full + 2 * PAD, half), f32)
    scratch = [
        boxes, boxes, boxes,
        pltpu.VMEM((4, nx + 1, strips, half, half), f32),
        pltpu.VMEM((nx + 1, strips, half, half), f32),
        pltpu.VMEM((nx + 1, strips, half, half), f32),
        pltpu.VMEM((2, nx + 1, half, half), f32),
        pltpu.VMEM((2, strips, half, half), f32),
        pltpu.VMEM((nx + 1, 2, 2, ny, PAD, half), f32),
        pltpu.VMEM((2, nx + 1, 2, 2, PAD, half), f32),
        pltpu.VMEM((height, full), f32),
        pltpu.VMEM((strips + 2, height, half), f32),
        pltpu.VMEM((2, nx + 1, half // 2 + PAD, half), f32),
        pltpu.VMEM((2, nx + 1, half // 2 + PAD, half), f32),
        pltpu.VMEM((2, PAD, half), f32),
        pltpu.VMEM((2, 2, PAD, half), f32),
        pltpu.SemaphoreType.DMA((nx, 2)),
        pltpu.SemaphoreType.DMA,
        pltpu.SemaphoreType.DMA((nx + 1, 2, 2)),
        pltpu.SemaphoreType.DMA((2, 2, nx + 1)),
        pltpu.SemaphoreType.DMA((2, 2, nx + 1)),
        pltpu.SemaphoreType.DMA((2, 2)),
        pltpu.SemaphoreType.DMA((2, 2)),
        pltpu.SemaphoreType.DMA((2, nx + 1)),
        pltpu.SemaphoreType.DMA((2, nx + 1)),
        pltpu.SemaphoreType.DMA((2,)),
        pltpu.SemaphoreType.DMA((2,)),
        pltpu.SemaphoreType.DMA((2,)),
        pltpu.SemaphoreType.DMA((2,)),
    ]
    return pl.pallas_call(
        make_kernel(nx, ny, size_x, size_y, half),
        out_shape=jax.ShapeDtypeStruct(basis.shape, f32),
        in_specs=[pl.BlockSpec(memory_space=pltpu.HBM)] * 2,
        out_specs=pl.BlockSpec(memory_space=pl.ANY),
        scratch_shapes=scratch,
        compiler_params=pltpu.CompilerParams(
            collective_id=0, has_side_effects=True, vmem_limit_bytes=48 * 1024 * 1024),
        name="smoothing",
    )(*[pltpu.with_memory_space_constraint(x, pltpu.HBM) for x in (permeability, basis)])


def solution(mesh):
    placed = (P("gx", "gy"), P("gx", "gy", None, None), P("gx", "gy", None, None))
    return jax.shard_map(
        local, mesh=mesh, in_specs=placed, out_specs=P("gx", "gy", None, None), check_vma=False
    )
```

```python
import jax
import jax.numpy as jnp
from jax import lax
from jax.experimental import pallas as pl
from jax.experimental.pallas import tpu as pltpu
from jax.sharding import PartitionSpec as P

MESH = pl.DeviceIdType.MESH
relaxation = 2.0 / 3.0
coupling = relaxation / (1.0 - relaxation)
PAD = 8
CH = 32
NEAR = 40


def pick(k, table):
    value = jnp.int32(table[-1])
    for n in range(len(table) - 2, -1, -1):
        value = jnp.where(k == n, table[n], value)
    return value


def first_needs(order, count):
    seen, out = set(), []
    for rb in order:
        new = [q for q in (rb - 1, rb, rb + 1) if 0 <= q < count and q not in seen]
        seen.update(new)
        out.append(new)
    return out


def make_kernel(nx, ny, size_x, size_y, half):
    full = 2 * half
    last = nx
    strips = ny + 1
    hw = half // 2

    pack_order = [1, 2, 0, nx - 1, nx - 2, nx] + list(range(3, nx - 2))
    weigh_order = [1, nx - 1] + list(range(2, nx - 1)) + [0, nx]
    assert sorted(weigh_order) == sorted(pack_order) == list(range(nx + 1))
    unpack_steps = first_needs(weigh_order, nx + 1)
    events, done, known = [], set(), set()
    for n, rb in enumerate(weigh_order):
        known.add(rb)
        allowed = list(range(1, nx)) + ([0, nx] if n >= nx - 1 else [])
        ready = [q for q in allowed if q not in done and {m for m in (q - 1, q, q + 1) if 0 <= m <= nx} <= known][:3]
        done.update(ready)
        events += [(rb, ready[0] if ready else -1)] + [(-1, q) for q in ready[1:]]
    assert sorted(q for _, q in events if q >= 0) == list(range(nx + 1))
    first_end = min(k for k, (_, q) in enumerate(events) if q in (0, nx))
    early = [n for n, _ in events].index(3)

    def kernel(*refs):
        (perm_h, basis_h, out_h,
         a, b, d, w, s, iv, rz, xrow, zrow, far, px, pm, pe, pk, pr, hk, hr,
         a_sem, p_sem, o_sem, zs_sem, zr_sem, gs_sem, gr_sem, cs_sem, cr_sem, fs_sem, fr_sem,
         ps_sem, pr_sem, hs_sem, hr_sem, rs_sem, rr_sem) = refs
        gx, gy = lax.axis_index("gx"), lax.axis_index("gy")
        has_up, has_down = gx > 0, gx < size_x - 1
        has_left, has_right = gy > 0, gy < size_y - 1
        up, down = (gx - 1, gy), (gx + 1, gy)
        left, right = (gx, gy - 1), (gx, gy + 1)
        z_sides = ((0, has_left, left), (1, has_right, right))
        x_sides = ((0, has_up, up), (1, has_down, down))
        halo = hw + PAD
        height = px.shape[0]
        length = height - 2 * halo

        def remote(src, dst, send, recv, target):
            return pltpu.make_async_remote_copy(
                src_ref=src, dst_ref=dst, send_sem=send, recv_sem=recv, device_id=target, device_id_type=MESH)

        def a_copy(i, h):
            return pltpu.make_async_copy(
                basis_h.at[i, :, :, pl.ds(h * half, half)], a.at[i + 1, :, h, pl.ds(PAD, full), :], a_sem.at[i, h])

        def o_copy(rb, part, h):
            lo = half if part == 0 else 0
            return pltpu.make_async_copy(
                d.at[rb + part, :, h, pl.ds(PAD + lo, half), :],
                out_h.at[rb - 1 + part, :, pl.ds(lo, half), pl.ds(h * half, half)], o_sem.at[rb, part, h])

        def row_copy(side, target):
            src, dst = (0, height - halo) if side == 0 else (length - halo, 0)
            return remote(perm_h.at[pl.ds(src, halo), :], px.at[pl.ds(dst, halo), :],
                          rs_sem.at[side], rr_sem.at[1 - side], target)

        def row_arrival(side, target):
            dst = 0 if side == 0 else height - halo
            return remote(perm_h.at[pl.ds(0, halo), :], px.at[pl.ds(dst, halo), :],
                          rs_sem.at[side], rr_sem.at[side], target)

        def pk_copy(side, target, rb):
            return remote(pk.at[side, rb], pr.at[1 - side, rb], ps_sem.at[side, rb], pr_sem.at[1 - side, rb], target)

        def pk_arrival(side, target, rb):
            return remote(pk.at[side, rb], pr.at[side, rb], ps_sem.at[side, rb], pr_sem.at[side, rb], target)

        def hk_copy(side, target):
            return remote(hk, hr.at[1 - side], hs_sem.at[side], hr_sem.at[1 - side], target)

        def hk_arrival(side, target):
            return remote(hk, hr.at[side], hs_sem.at[side], hr_sem.at[side], target)

        def z_copy(side, target, rb):
            strip = 0 if side == 0 else strips - 1
            return remote(s.at[rb, strip], rz.at[1 - side, rb], zs_sem.at[side, rb], zr_sem.at[1 - side, rb], target)

        def z_arrival(side, target, rb):
            return remote(s.at[rb, 0], rz.at[side, rb], zs_sem.at[side, rb], zr_sem.at[side, rb], target)

        def g_copy(side, target, h):
            i, lo, to = (0, 0, nx + 1) if side == 0 else (nx - 1, half - PAD, 0)
            return remote(basis_h.at[i, :, pl.ds(lo, half + PAD), pl.ds(h * half, half)],
                          a.at[to, :, h, pl.ds(PAD + lo, half + PAD), :],
                          gs_sem.at[side, h], gr_sem.at[1 - side, h], target)

        def g_arrival(side, target, h):
            lo, to = (half - PAD, 0) if side == 0 else (0, nx + 1)
            return remote(basis_h.at[0, :, pl.ds(0, half + PAD), pl.ds(h * half, half)],
                          a.at[to, :, h, pl.ds(PAD + lo, half + PAD), :],
                          gs_sem.at[side, h], gr_sem.at[side, h], target)

        def c_copy(side, target):
            i, lo = (2, PAD) if side == 0 else (nx - 1, full)
            return remote(b.at[i, :, :, pl.ds(lo, PAD), :], xrow.at[1 - side], cs_sem.at[side], cr_sem.at[1 - side], target)

        def c_arrival(side, target):
            return remote(b.at[2, :, :, pl.ds(PAD, PAD), :], xrow.at[side], cs_sem.at[side], cr_sem.at[side], target)

        def f_copy(side, target, end):
            j, h = (0, 0) if side == 0 else (ny - 1, 1)
            return remote(xrow.at[end, j, h], zrow.at[1 - side, end], fs_sem.at[side, end], fr_sem.at[1 - side, end], target)

        def f_arrival(side, target, end):
            return remote(xrow.at[end, 0, 0], zrow.at[side, end], fs_sem.at[side, end], fr_sem.at[side, end], target)

        def each(sides, act):
            for side, has, target in sides:
                @pl.when(has)
                def _():
                    act(side, target)

        barrier = pltpu.get_barrier_semaphore()
        each(z_sides + x_sides, lambda side, target: pl.semaphore_signal(
            barrier, inc=1, device_id=target, device_id_type=MESH))

        own = pltpu.make_async_copy(perm_h, px.at[pl.ds(halo, length), :], p_sem)
        own.start()

        @pl.loop(0, nx)
        def _(k):
            i = pick(k, [0, nx - 1, 1, nx - 2] + list(range(2, nx - 2)))
            a_copy(i, 0).start()
            a_copy(i, 1).start()

        edge = jnp.zeros((PAD, half), jnp.float32)

        @pl.loop(0, nx)
        def _(i):
            for buf in (a, b):
                for j in range(ny):
                    for h in range(2):
                        buf[i + 1, j, h, 0:PAD, :] = edge
                        buf[i + 1, j, h, PAD + full:, :] = edge

        for buf in (a, b):
            for j in range(ny):
                for h in range(2):
                    buf[0, j, h, PAD + full:, :] = edge
                    buf[nx + 1, j, h, 0:PAD, :] = edge

        far[...] = jnp.zeros(far.shape, jnp.float32)
        for j in range(ny):
            for h in range(2):
                b[0, j, h, half:half + PAD, :] = edge
                b[nx + 1, j, h, PAD + half:2 * PAD + half, :] = edge

        for side, has, _t in z_sides:
            @pl.when(jnp.logical_not(has))
            def _():
                @pl.loop(0, nx + 1)
                def _(rb):
                    rz[side, rb] = jnp.zeros((half + PAD, half), jnp.float32)
                    pr[side, rb] = jnp.zeros((hw + PAD, half), jnp.float32)
                hr[side] = jnp.zeros((2, PAD, half), jnp.float32)
                zrow[side] = jnp.zeros((2, PAD, half), jnp.float32)

        for side, has, _t in x_sides:
            @pl.when(jnp.logical_not(has))
            def _():
                lo = 0 if side == 0 else height - halo
                px[lo:lo + halo, :] = jnp.zeros((halo, full), jnp.float32)
                lo, to = (half, 0) if side == 0 else (PAD, nx + 1)
                for j in range(ny):
                    for h in range(2):
                        a[to, j, h, lo:lo + half + PAD, :] = jnp.zeros((half + PAD, half), jnp.float32)
                xrow[side] = jnp.zeros((ny, 2, PAD, half), jnp.float32)

                for z, has_z, _z in z_sides:
                    @pl.when(has_z)
                    def _():
                        zrow[z, side] = edge

        lane = lax.broadcasted_iota(jnp.int32, (hw, half), 1)
        low_half = lane < hw
        lane8 = lax.broadcasted_iota(jnp.int32, (PAD, half), 1)

        def shifted_rows(lo, count):
            return pltpu.roll(px[pl.ds(lo, count), :], hw, 1)

        def pack(rb):
            lo = pl.multiple_of(rb * half + PAD, PAD)
            first = shifted_rows(lo, hw)
            second = shifted_rows(lo + hw, hw)
            m0, m1 = first[:, :half], second[:, :half]
            for n, part in ((0, first), (1, second)):
                pm[pl.ds(lo + n * hw, hw), :] = part[:, :half]
                pe[2, pl.ds(lo + n * hw, hw), :] = part[:, half:]
            pk[1, rb, 0:hw, :] = jnp.where(low_half, m0, pltpu.roll(m1, hw, 1))
            pk[0, rb, 0:hw, :] = jnp.where(low_half, pltpu.roll(m0, hw, 1), m1)
            to_left = jnp.zeros((PAD, half), jnp.float32)
            to_right = to_left
            for k in range(half // PAD):
                part = first if k * PAD < hw else second
                q = k * PAD % hw
                e = part[q:q + PAD, half:]
                here = lane8 == k
                to_left = jnp.where(here, pltpu.roll(e, k, 1) if k else e, to_left)
                to_right = jnp.where(here, pltpu.roll(e, k + 1, 1), to_right)
            pk[0, rb, hw:hw + PAD, :] = to_left
            pk[1, rb, hw:hw + PAD, :] = to_right
            each(z_sides, lambda side, target: pk_copy(side, target, rb).start())

        ends = ((0, 0), (1, height - PAD))

        def pack_ends():
            for n, lo in ends:
                rolled = shifted_rows(lo, PAD)
                hk[n] = rolled[:, :half]
                pm[lo:lo + PAD, :] = rolled[:, :half]
                pe[2, lo:lo + PAD, :] = rolled[:, half:]
            each(z_sides, lambda side, target: hk_copy(side, target).start())

        def unpack(rb):
            each(z_sides, lambda side, target: pk_arrival(side, target, rb).wait_recv())
            lo = pl.multiple_of(rb * half + PAD, PAD)
            from_left, from_right = pr[0, rb, 0:hw, :], pr[1, rb, 0:hw, :]
            for n in range(2):
                start = lo + n * hw
                m = pm[pl.ds(start, hw), :]
                fl = pltpu.roll(from_left, hw, 1) if n else from_left
                fr = from_right if n else pltpu.roll(from_right, hw, 1)
                pe[1, pl.ds(start, hw), :] = jnp.where(low_half, fl, m)
                pe[3, pl.ds(start, hw), :] = jnp.where(low_half, m, fr)
            cl, cr = pr[0, rb, hw:hw + PAD, :], pr[1, rb, hw:hw + PAD, :]
            for k in range(half // PAD):
                pe[0, pl.ds(lo + k * PAD, PAD), :] = pltpu.roll(cl, half - 1 - k, 1)
                pe[4, pl.ds(lo + k * PAD, PAD), :] = pltpu.roll(cr, half - k, 1) if k else cr

        def unpack_ends():
            each(z_sides, lambda side, target: hk_arrival(side, target).wait_recv())
            low8 = lane8 < hw
            for n, lo in ends:
                pe[1, lo:lo + PAD, :] = jnp.where(low8, hr[0, n], hk[n])
                pe[3, lo:lo + PAD, :] = jnp.where(low8, hk[n], hr[1, n])

        lane_h = lax.broadcasted_iota(jnp.int32, (CH, half), 1)
        row_h = lax.broadcasted_iota(jnp.int32, (CH, half), 0)
        first_lane, last_lane = lane_h == 0, lane_h == half - 1

        def ahead(x):
            return pltpu.roll(x, half - 1, 1)

        def behind(x):
            return pltpu.roll(x, 1, 1)

        def weigh(rb, chosen):
            base = pl.multiple_of(rb * half + PAD, PAD)
            for r in range(0, half, CH):
                for c in chosen:
                    inner = 0 < c < strips - 1
                    mid = pe[c + 1, pl.ds(base + r, CH), :]
                    after = pm[pl.ds(base + r, CH), :] if inner else pe[c + 2, pl.ds(base + r, CH), :]
                    before = after if inner else pe[c, pl.ds(base + r, CH), :]
                    east = pe[c + 1, pl.ds(base + r + 1, CH), :]
                    west = pe[c + 1, pl.ds(base + r - 1, CH), :]
                    north = ahead(jnp.where(first_lane, after, mid))
                    south = behind(jnp.where(last_lane, before, mid))
                    se, sw, sn, ss = mid + east, mid + west, mid + north, mid + south
                    across, along = sn * ss, se * sw
                    ne, nw = east * sw * across, west * se * across
                    nn, ns = north * ss * along, south * sn * along
                    scale = coupling / jnp.maximum((ne + nw) + (nn + ns), 1e-30)
                    for n, face in enumerate((ne, nw, nn, ns)):
                        w[n, rb, c, r:r + CH, :] = face * scale

        def accumulate(store, c, value):
            store[c] = value if store[c] is None else store[c] + value

        def update(src, rb, r, part, j):
            lo = PAD + r + (half if part == 0 else 0)
            xs = [src[rb + part, j, h, lo:lo + CH, :] for h in range(2)]
            fores, afts = [ahead(x) for x in xs], [behind(x) for x in xs]
            fore = (jnp.where(last_lane, fores[1], fores[0]), jnp.where(last_lane, 0.0, fores[1]))
            aft = (jnp.where(first_lane, 0.0, afts[0]), jnp.where(first_lane, afts[0], afts[1]))
            news = []
            for h in range(2):
                c = j + h
                new = xs[h] + w[0, rb, c, r:r + CH, :] * src[rb + part, j, h, lo + 1:lo + 1 + CH, :]
                new = new + w[1, rb, c, r:r + CH, :] * src[rb + part, j, h, lo - 1:lo - 1 + CH, :]
                new = new + w[2, rb, c, r:r + CH, :] * fore[h]
                news.append(new + w[3, rb, c, r:r + CH, :] * aft[h])
            return lo, xs, news, fores[1], afts[1], fores[0], afts

        def smooth_first(rb, chosen):
            for r in range(0, half, CH):
                for c in chosen:
                    total = [None]
                    faces = [w[n, rb, c, r:r + CH, :] for n in range(4)]
                    for j, h in ((c - 1, 1), (c, 0)):
                        if not 0 <= j < ny:
                            continue
                        for part in range(2):
                            lo = PAD + r + (half if part == 0 else 0)
                            x = a[rb + part, j, h, lo:lo + CH, :]
                            beside = a[rb + part, j, 1 - h, lo:lo + CH, :]
                            fore = ahead(jnp.where(first_lane, beside if h == 0 else 0.0, x))
                            aft = behind(jnp.where(last_lane, beside if h == 1 else 0.0, x))
                            new = x + faces[0] * a[rb + part, j, h, lo + 1:lo + 1 + CH, :]
                            new = new + faces[1] * a[rb + part, j, h, lo - 1:lo - 1 + CH, :]
                            new = new + faces[2] * fore + faces[3] * aft
                            value = jnp.where(x > 0, new, 0.0)
                            b[rb + part, j, h, lo:lo + CH, :] = value
                            accumulate(total, 0, value)
                    s[rb, c, r:r + CH, :] = total[0]

        def normalise(rb):
            each(z_sides, lambda side, target: z_arrival(side, target, rb).wait_recv())
            for c in range(strips):
                for r in range(0, half, CH):
                    total = s[rb, c, r:r + CH, :]
                    if c == 0:
                        total = total + rz[0, rb, r:r + CH, :]
                    if c == strips - 1:
                        total = total + rz[1, rb, r:r + CH, :]
                    scale = 1.0 / jnp.where(total > 0, total, 1.0)
                    for z, strip in ((0, 0), (1, strips - 1)):
                        if c == strip:
                            iv[z, pl.ds(pl.multiple_of(rb * half + PAD, PAD) + r, CH), :] = scale
                    for j, h in ((c - 1, 1), (c, 0)):
                        if 0 <= j < ny:
                            for part in range(2):
                                lo = PAD + r + (half if part == 0 else 0)
                                b[rb + part, j, h, lo:lo + CH, :] = b[rb + part, j, h, lo:lo + CH, :] * scale

        row_near = lax.broadcasted_iota(jnp.int32, (NEAR, half), 0)
        lane_1 = lax.broadcasted_iota(jnp.int32, (1, half), 1)
        lane_f = lane_1.astype(jnp.float32)

        def record(rb):
            for side in range(2):
                j, strip = (0, 0) if side == 0 else (ny - 1, strips - 1)
                rim_lane = 0 if side == 0 else half - 1
                rim_row = 0 if side == 0 else NEAR - 1

                def turn(value):
                    turned = jnp.transpose(value)
                    return turned[0:NEAR] if side == 0 else turned[half - NEAR:]

                rim, places, lanes = None, [], []
                for part in range(2):
                    off = PAD + (half if part == 0 else 0)
                    inside = jnp.where(a[rb + part, j, side, PAD + half - part * PAD:PAD + half - part * PAD + 1, :] > 0, 1.0, 0.0)
                    inside = jnp.sum(inside, axis=1, keepdims=True)
                    place = (half - 1.0) - inside if side == 0 else inside
                    taken = jnp.logical_or(lane_f == (place + 1.0 if side == 0 else place - 1.0), lane_1 == rim_lane)
                    turned = turn(jnp.where(taken, b[rb + part, j, side, off:off + half, :], 0.0))
                    s[rb, strip, half + part:half + part + 1, :] = jnp.sum(
                        jnp.where(row_near == rim_row, 0.0, turned), axis=0, keepdims=True)
                    value = turned[rim_row:rim_row + 1]
                    rim = value if rim is None else rim + value
                    q = off + half - NEAR if part == 0 else off
                    beside = 1 if part == 0 else -1
                    near = b[rb + part, j, side, q:q + NEAR, :]
                    here = a[rb + part, j, side, q:q + NEAR, :]
                    over = a[rb + part, j, side, q + beside:q + beside + NEAR, :]
                    count = jnp.sum(jnp.where(here > 0, 1.0, 0.0), axis=0, keepdims=True)
                    inner = count[:, half - 1:] if side == 0 else count[:, 0:1]
                    places.append(inner + (half - NEAR) if part == 0 else (NEAR - 1) - inner)
                    lanes.append(place)
                    s[rb, strip, half + 2 + part:half + 3 + part, :] = jnp.sum(jnp.where(over > 0, 0.0, near), axis=0, keepdims=True)
                other, beside = (1, 1) if side == 0 else (ny - 2, strips - 2)
                both = b[rb, other, side, PAD + half:PAD + full, :] + b[rb + 1, other, side, PAD:PAD + half, :]
                total = s[rb, beside, 0:half, :]
                both = jnp.where(lane_1 == rim_lane, both / jnp.where(total > 0, total, 1.0), 0.0)
                s[rb, strip, half + 4:half + 5, :] = turn(both)[rim_row:rim_row + 1]
                s[rb, strip, half + 5:half + 6, :] = rim
                where = jnp.zeros((1, half), jnp.float32)
                for n, value in enumerate(places + lanes):
                    where = jnp.where(lane_1 == n, value, where)
                s[rb, strip, half + 6:half + 7, :] = where
                s[rb, strip, half + 7:, :] = jnp.zeros((1, half), jnp.float32)

        def spread(value, r):
            return jnp.sum(jnp.where(lane_h == row_h + r, value, 0.0), axis=1, keepdims=True)

        row_f = row_h.astype(jnp.float32)
        lane_hf = lane_h.astype(jnp.float32)

        def finish(rb):
            inner_up, inner_down = rb > 0, rb < nx
            base = pl.multiple_of(rb * half + PAD, PAD)

            def where_of(z, q):
                line = rz[z, q, half + 6:half + 7, :]
                return [line[:, n:n + 1] for n in range(4)]

            spots = [where_of(z, rb) for z in range(2)]
            for r in range(0, half, CH):
                lost = [None] * strips
                results = [[] for _ in range(strips)]
                for part in range(2):
                    for j in range(ny):
                        lo, xs, news, _, aft_end, fore_start, _a = update(b, rb, r, part, j)
                        for h in range(2):
                            mask = a[rb + part, j, h, lo:lo + CH, :] > 0
                            results[j + h].append((part, j, h, lo, jnp.where(mask, news[h], 0.0)))
                            accumulate(lost, j + h, jnp.where(mask, 0.0, news[h]))
                        if j + 2 < strips:
                            accumulate(lost, j + 2, w[3, rb, j + 2, r:r + CH, :] * jnp.where(first_lane, aft_end, 0.0))
                        if j >= 1:
                            accumulate(lost, j - 1, w[2, rb, j - 1, r:r + CH, :] * jnp.where(last_lane, fore_start, 0.0))
                for part, row, inner in ((0, 0, inner_up), (1, half - 1, inner_down)):
                    if r <= row < r + CH:
                        for c in range(strips):
                            over = [None]
                            for j, h, z in ((c - 1, 1, 0), (c, 0, 1)):
                                if part == 0:
                                    i, at, q = jnp.maximum(rb - 1, 0), PAD + full - 1, jnp.maximum(rb - 1, 0)
                                else:
                                    i, at, q = jnp.minimum(rb + 2, nx + 1), PAD, jnp.minimum(rb + 1, nx)
                                if 0 <= j < ny:
                                    accumulate(over, 0, b[i, j, h, at:at + 1, :])
                                else:
                                    spot = rz[z, q, half + 6:half + 7, part:part + 1]
                                    there = iv[z, pl.ds(base + (-1 if part == 0 else half), 1), :]
                                    value = rz[z, q, half + 2 + part:half + 3 + part, :] * there
                                    accumulate(over, 0, jnp.where(spot == (half if part == 0 else -1), value, 0.0))
                            keep = jnp.logical_and(row_h + r == row, inner)
                            accumulate(lost, c, w[1 - part, rb, c, r:r + CH, :] * jnp.where(keep, over[0], 0.0))
                for z, side, c in ((0, 1, 0), (1, 0, strips - 1)):
                    at_rim = last_lane if side == 0 else first_lane
                    face = 2 if side == 0 else 3
                    scale = iv[z, pl.ds(base + r, CH), :]
                    shifted = ahead(scale) if side == 0 else behind(scale)
                    v = [spread(rz[z, rb, half + n:half + n + 1, :], r) for n in (0, 1, 4, 5)]
                    field = jnp.where(lane_hf == spots[z][2], v[0], 0.0) + jnp.where(lane_hf == spots[z][3], v[1], 0.0)
                    field = field * shifted + jnp.where(at_rim, v[2], 0.0)
                    accumulate(lost, c, w[face, rb, c, r:r + CH, :] * field)
                    other = c + (1 if side == 1 else -1)
                    accumulate(lost, other, w[face, rb, other, r:r + CH, :] * jnp.where(at_rim, v[3] * shifted, 0.0))
                    for part in range(2):
                        if (r + CH > half - NEAR) if part == 0 else (r < NEAR):
                            line = jnp.where(row_f + r == spots[z][part], rz[z, rb, half + 2 + part:half + 3 + part, :], 0.0)
                            there = iv[z, pl.ds(base + r + (-1 if part == 0 else 1), CH), :]
                            accumulate(lost, c, w[1 - part, rb, c, r:r + CH, :] * line * there)
                for c in range(strips):
                    extra = ends_lost(rb, c, r)
                    total = (1.0 + coupling) - (lost[c] if extra is None else lost[c] + extra)
                    scale = 1.0 / total
                    for part, j, h, lo, value in results[c]:
                        d[rb + part, j, h, lo:lo + CH, :] = value * scale

        def ends_lost(rb, c, r):
            for end, row in ((0, 0), (1, half - 1)):
                if r <= row < r + CH:
                    keep = jnp.logical_and(row_h + r == row, rb == (0 if end == 0 else nx))
                    return w[1 - end, rb, c, r:r + CH, :] * jnp.where(keep, far[end, c, 0:1, :], 0.0)
            return None

        def gather_far():
            for end in range(2):
                at = PAD - 1 if end == 0 else 0
                for c in range(strips):
                    over = [None]
                    for j, h, z in ((c - 1, 1, 0), (c, 0, 1)):
                        accumulate(over, 0, xrow[end, j, h, at:at + 1, :] if 0 <= j < ny else zrow[z, end, at:at + 1, :])
                    far[end, c, 0:1, :] = over[0]

        def o_each(rb, act):
            for part, inside in ((0, rb > 0), (1, rb < nx)):
                @pl.when(inside)
                def _():
                    for h in range(2):
                        act(o_copy(rb, part, h))

        peers = sum(jnp.where(has, 1, 0) for _, has, _t in z_sides + x_sides)
        pl.semaphore_wait(barrier, peers)

        each(x_sides, lambda side, target: row_copy(side, target).start())

        def send_boxes(side, target):
            for h in range(2):
                g_copy(side, target, h).start()
        each(x_sides, send_boxes)
        own.wait()

        @pl.loop(0, nx + 1)
        def _(k):
            rb = pick(k, pack_order)

            @pl.when(rb == 0)
            def _():
                each(x_sides, lambda side, target: row_arrival(side, target).wait_recv())
                pack_ends()

            pack(rb)

        @pl.loop(0, nx)
        def _(i):
            a_copy(i, 0).wait()
            a_copy(i, 1).wait()

        inner_strips, outer_strips = list(range(1, strips - 1)), [0, strips - 1]

        @pl.loop(1, nx)
        def _(rb):
            weigh(rb, inner_strips)
            smooth_first(rb, inner_strips)

        for n, rb in enumerate(unpack_steps[0]):
            unpack(rb)
        unpack_ends()
        width = max(len(n) for n in unpack_steps[1:])

        @pl.loop(0, nx + 1)
        def _(k):
            rb = pick(k, weigh_order)
            for q in range(width):
                new = pick(k, [-1] + [n[q] if q < len(n) else -1 for n in unpack_steps[1:]])

                @pl.when(new >= 0)
                def _():
                    unpack(new)

            weigh(rb, outer_strips)

            @pl.when(jnp.logical_or(rb == 0, rb == nx))
            def _():
                for side, at in ((0, 0), (1, nx)):
                    @pl.when(rb == at)
                    def _():
                        _, has, target = x_sides[side]

                        @pl.when(has)
                        def _():
                            for h in range(2):
                                g_arrival(side, target, h).wait_recv()
                weigh(rb, inner_strips)
                smooth_first(rb, inner_strips)

            smooth_first(rb, outer_strips)
            record(rb)
            each(z_sides, lambda side, target: z_copy(side, target, rb).start())

        @pl.loop(0, len(events))
        def _(k):
            rb = pick(k, [n for n, _ in events])

            @pl.when(rb >= 0)
            def _():
                normalise(rb)
                for side, at in ((0, 1), (1, nx - 1)):
                    @pl.when(rb == at)
                    def _():
                        _, has, target = x_sides[side]

                        @pl.when(has)
                        def _():
                            c_copy(side, target).start()

            @pl.when(k == early)
            def _():
                def forward(end, target):
                    c_copy(end, target).wait_send()
                    c_arrival(end, target).wait_recv()
                    each(z_sides, lambda side, to: f_copy(side, to, end).start())
                each(x_sides, forward)

            now = pick(k, [n for _, n in events])

            @pl.when(k == first_end)
            def _():
                each(x_sides, lambda end, target: each(z_sides, lambda side, to: f_arrival(side, to, end).wait_recv()))
                gather_far()

            @pl.when(now >= 0)
            def _():
                finish(now)
                o_each(now, lambda copy: copy.start())

        @pl.loop(0, nx + 1)
        def _(rb):
            o_each(rb, lambda copy: copy.wait())

        def drain(side, target):
            @pl.loop(0, nx + 1)
            def _(rb):
                z_copy(side, target, rb).wait_send()
                pk_copy(side, target, rb).wait_send()
            hk_copy(side, target).wait_send()
        each(z_sides, drain)

        def drain_rows(end, target):
            row_copy(end, target).wait_send()
            for h in range(2):
                g_copy(end, target, h).wait_send()
            each(z_sides, lambda side, to: f_copy(side, to, end).wait_send())
        each(x_sides, drain_rows)

    return kernel


def local(permeability, basis, support):
    nx, ny, full, _ = basis.shape
    half = full // 2
    size_x, size_y = lax.axis_size("gx"), lax.axis_size("gy")
    height = permeability.shape[0] + half + 2 * PAD
    f32 = jnp.float32
    strips = ny + 1
    boxes = pltpu.VMEM((nx + 2, ny, 2, full + 2 * PAD, half), f32)
    scratch = [
        boxes, boxes, boxes,
        pltpu.VMEM((4, nx + 1, strips, half, half), f32),
        pltpu.VMEM((nx + 1, strips, half + PAD, half), f32),
        pltpu.VMEM((2, (nx + 1) * half + 2 * PAD, half), f32),
        pltpu.VMEM((2, nx + 1, half + PAD, half), f32),
        pltpu.VMEM((2, ny, 2, PAD, half), f32),
        pltpu.VMEM((2, 2, PAD, half), f32),
        pltpu.VMEM((2, strips, PAD, half), f32),
        pltpu.VMEM((height, full), f32),
        pltpu.VMEM((height, half), f32),
        pltpu.VMEM((strips + 2, height, half), f32),
        pltpu.VMEM((2, nx + 1, half // 2 + PAD, half), f32),
        pltpu.VMEM((2, nx + 1, half // 2 + PAD, half), f32),
        pltpu.VMEM((2, PAD, half), f32),
        pltpu.VMEM((2, 2, PAD, half), f32),
        pltpu.SemaphoreType.DMA((nx, 2)),
        pltpu.SemaphoreType.DMA,
        pltpu.SemaphoreType.DMA((nx + 1, 2, 2)),
        pltpu.SemaphoreType.DMA((2, nx + 1)),
        pltpu.SemaphoreType.DMA((2, nx + 1)),
        pltpu.SemaphoreType.DMA((2, 2)),
        pltpu.SemaphoreType.DMA((2, 2)),
        pltpu.SemaphoreType.DMA((2,)),
        pltpu.SemaphoreType.DMA((2,)),
        pltpu.SemaphoreType.DMA((2, 2)),
        pltpu.SemaphoreType.DMA((2, 2)),
        pltpu.SemaphoreType.DMA((2, nx + 1)),
        pltpu.SemaphoreType.DMA((2, nx + 1)),
        pltpu.SemaphoreType.DMA((2,)),
        pltpu.SemaphoreType.DMA((2,)),
        pltpu.SemaphoreType.DMA((2,)),
        pltpu.SemaphoreType.DMA((2,)),
    ]
    return pl.pallas_call(
        make_kernel(nx, ny, size_x, size_y, half),
        out_shape=jax.ShapeDtypeStruct(basis.shape, f32),
        in_specs=[pl.BlockSpec(memory_space=pltpu.HBM)] * 2,
        out_specs=pl.BlockSpec(memory_space=pl.ANY),
        scratch_shapes=scratch,
        compiler_params=pltpu.CompilerParams(
            collective_id=0, has_side_effects=True, vmem_limit_bytes=48 * 1024 * 1024),
        name="smoothing",
    )(*[pltpu.with_memory_space_constraint(x, pltpu.HBM) for x in (permeability, basis)])


def solution(mesh):
    placed = (P("gx", "gy"), P("gx", "gy", None, None), P("gx", "gy", None, None))
    return jax.shard_map(
        local, mesh=mesh, in_specs=placed, out_specs=P("gx", "gy", None, None), check_vma=False
    )
```

```python
import jax
import jax.numpy as jnp
from jax import lax
from jax.experimental import pallas as pl
from jax.experimental.pallas import tpu as pltpu
from jax.sharding import PartitionSpec as P

MESH = pl.DeviceIdType.MESH
relaxation = 2.0 / 3.0
coupling = relaxation / (1.0 - relaxation)
PAD = 8
CH = 64
NEAR = 40


def pick(k, table):
    value = jnp.int32(table[-1])
    for n in range(len(table) - 2, -1, -1):
        value = jnp.where(k == n, table[n], value)
    return value


def first_needs(order, count):
    seen, out = set(), []
    for rb in order:
        new = [q for q in (rb - 1, rb, rb + 1) if 0 <= q < count and q not in seen]
        seen.update(new)
        out.append(new)
    return out


def make_kernel(nx, ny, size_x, size_y, half):
    full = 2 * half
    last = nx
    strips = ny + 1
    hw = half // 2

    pack_order = [1, 2, 0, nx - 1, nx - 2, nx] + list(range(3, nx - 2))
    weigh_order = [1, nx - 1] + list(range(2, nx - 1)) + [0, nx]
    assert sorted(weigh_order) == sorted(pack_order) == list(range(nx + 1))
    unpack_steps = first_needs(weigh_order, nx + 1)
    events, done, known = [], set(), set()
    for n, rb in enumerate(weigh_order):
        known.add(rb)
        allowed = list(range(1, nx)) + ([0, nx] if n >= nx - 1 else [])
        ready = [q for q in allowed if q not in done and {m for m in (q - 1, q, q + 1) if 0 <= m <= nx} <= known][:3]
        done.update(ready)
        events += [(rb, ready[0] if ready else -1)] + [(-1, q) for q in ready[1:]]
    assert sorted(q for _, q in events if q >= 0) == list(range(nx + 1))
    first_end = min(k for k, (_, q) in enumerate(events) if q in (0, nx))
    early = [n for n, _ in events].index(3)

    def kernel(*refs):
        (perm_h, basis_h, out_h,
         a, b, d, w, s, iv, rz, xrow, zrow, far, px, pm, pe, pk, pr, hk, hr,
         a_sem, p_sem, o_sem, zs_sem, zr_sem, gs_sem, gr_sem, cs_sem, cr_sem, fs_sem, fr_sem,
         ps_sem, pr_sem, hs_sem, hr_sem, rs_sem, rr_sem) = refs
        gx, gy = lax.axis_index("gx"), lax.axis_index("gy")
        has_up, has_down = gx > 0, gx < size_x - 1
        has_left, has_right = gy > 0, gy < size_y - 1
        up, down = (gx - 1, gy), (gx + 1, gy)
        left, right = (gx, gy - 1), (gx, gy + 1)
        z_sides = ((0, has_left, left), (1, has_right, right))
        x_sides = ((0, has_up, up), (1, has_down, down))
        halo = hw + PAD
        height = px.shape[0]
        length = height - 2 * halo

        def remote(src, dst, send, recv, target):
            return pltpu.make_async_remote_copy(
                src_ref=src, dst_ref=dst, send_sem=send, recv_sem=recv, device_id=target, device_id_type=MESH)

        def a_copy(i, h):
            return pltpu.make_async_copy(
                basis_h.at[i, :, :, pl.ds(h * half, half)], a.at[i + 1, :, h, pl.ds(PAD, full), :], a_sem.at[i, h])

        def o_copy(rb, part, h):
            lo = half if part == 0 else 0
            return pltpu.make_async_copy(
                d.at[rb + part, :, h, pl.ds(PAD + lo, half), :],
                out_h.at[rb - 1 + part, :, pl.ds(lo, half), pl.ds(h * half, half)], o_sem.at[rb, part, h])

        def row_copy(side, target):
            src, dst = (0, height - halo) if side == 0 else (length - halo, 0)
            return remote(perm_h.at[pl.ds(src, halo), :], px.at[pl.ds(dst, halo), :],
                          rs_sem.at[side], rr_sem.at[1 - side], target)

        def row_arrival(side, target):
            dst = 0 if side == 0 else height - halo
            return remote(perm_h.at[pl.ds(0, halo), :], px.at[pl.ds(dst, halo), :],
                          rs_sem.at[side], rr_sem.at[side], target)

        def pk_copy(side, target, rb):
            return remote(pk.at[side, rb], pr.at[1 - side, rb], ps_sem.at[side, rb], pr_sem.at[1 - side, rb], target)

        def pk_arrival(side, target, rb):
            return remote(pk.at[side, rb], pr.at[side, rb], ps_sem.at[side, rb], pr_sem.at[side, rb], target)

        def hk_copy(side, target):
            return remote(hk, hr.at[1 - side], hs_sem.at[side], hr_sem.at[1 - side], target)

        def hk_arrival(side, target):
            return remote(hk, hr.at[side], hs_sem.at[side], hr_sem.at[side], target)

        def z_copy(side, target, rb):
            strip = 0 if side == 0 else strips - 1
            return remote(s.at[rb, strip], rz.at[1 - side, rb], zs_sem.at[side, rb], zr_sem.at[1 - side, rb], target)

        def z_arrival(side, target, rb):
            return remote(s.at[rb, 0], rz.at[side, rb], zs_sem.at[side, rb], zr_sem.at[side, rb], target)

        def g_copy(side, target, h):
            i, lo, to = (0, 0, nx + 1) if side == 0 else (nx - 1, half - PAD, 0)
            return remote(basis_h.at[i, :, pl.ds(lo, half + PAD), pl.ds(h * half, half)],
                          a.at[to, :, h, pl.ds(PAD + lo, half + PAD), :],
                          gs_sem.at[side, h], gr_sem.at[1 - side, h], target)

        def g_arrival(side, target, h):
            lo, to = (half - PAD, 0) if side == 0 else (0, nx + 1)
            return remote(basis_h.at[0, :, pl.ds(0, half + PAD), pl.ds(h * half, half)],
                          a.at[to, :, h, pl.ds(PAD + lo, half + PAD), :],
                          gs_sem.at[side, h], gr_sem.at[side, h], target)

        def c_copy(side, target):
            i, lo = (2, PAD) if side == 0 else (nx - 1, full)
            return remote(b.at[i, :, :, pl.ds(lo, PAD), :], xrow.at[1 - side], cs_sem.at[side], cr_sem.at[1 - side], target)

        def c_arrival(side, target):
            return remote(b.at[2, :, :, pl.ds(PAD, PAD), :], xrow.at[side], cs_sem.at[side], cr_sem.at[side], target)

        def f_copy(side, target, end):
            j, h = (0, 0) if side == 0 else (ny - 1, 1)
            return remote(xrow.at[end, j, h], zrow.at[1 - side, end], fs_sem.at[side, end], fr_sem.at[1 - side, end], target)

        def f_arrival(side, target, end):
            return remote(xrow.at[end, 0, 0], zrow.at[side, end], fs_sem.at[side, end], fr_sem.at[side, end], target)

        def each(sides, act):
            for side, has, target in sides:
                @pl.when(has)
                def _():
                    act(side, target)

        barrier = pltpu.get_barrier_semaphore()
        each(z_sides + x_sides, lambda side, target: pl.semaphore_signal(
            barrier, inc=1, device_id=target, device_id_type=MESH))

        own = pltpu.make_async_copy(perm_h, px.at[pl.ds(halo, length), :], p_sem)
        own.start()

        @pl.loop(0, nx)
        def _(k):
            i = pick(k, [0, nx - 1, 1, nx - 2] + list(range(2, nx - 2)))
            a_copy(i, 0).start()
            a_copy(i, 1).start()

        edge = jnp.zeros((PAD, half), jnp.float32)

        @pl.loop(0, nx)
        def _(i):
            for buf in (a, b):
                for j in range(ny):
                    for h in range(2):
                        buf[i + 1, j, h, 0:PAD, :] = edge
                        buf[i + 1, j, h, PAD + full:, :] = edge

        for buf in (a, b):
            for j in range(ny):
                for h in range(2):
                    buf[0, j, h, PAD + full:, :] = edge
                    buf[nx + 1, j, h, 0:PAD, :] = edge

        far[...] = jnp.zeros(far.shape, jnp.float32)
        for j in range(ny):
            for h in range(2):
                b[0, j, h, half:half + PAD, :] = edge
                b[nx + 1, j, h, PAD + half:2 * PAD + half, :] = edge

        for side, has, _t in z_sides:
            @pl.when(jnp.logical_not(has))
            def _():
                @pl.loop(0, nx + 1)
                def _(rb):
                    rz[side, rb] = jnp.zeros((half + PAD, half), jnp.float32)
                    pr[side, rb] = jnp.zeros((hw + PAD, half), jnp.float32)
                hr[side] = jnp.zeros((2, PAD, half), jnp.float32)
                zrow[side] = jnp.zeros((2, PAD, half), jnp.float32)

        for side, has, _t in x_sides:
            @pl.when(jnp.logical_not(has))
            def _():
                lo = 0 if side == 0 else height - halo
                px[lo:lo + halo, :] = jnp.zeros((halo, full), jnp.float32)
                lo, to = (half, 0) if side == 0 else (PAD, nx + 1)
                for j in range(ny):
                    for h in range(2):
                        a[to, j, h, lo:lo + half + PAD, :] = jnp.zeros((half + PAD, half), jnp.float32)
                xrow[side] = jnp.zeros((ny, 2, PAD, half), jnp.float32)

                for z, has_z, _z in z_sides:
                    @pl.when(has_z)
                    def _():
                        zrow[z, side] = edge

        lane = lax.broadcasted_iota(jnp.int32, (hw, half), 1)
        low_half = lane < hw
        lane8 = lax.broadcasted_iota(jnp.int32, (PAD, half), 1)

        def shifted_rows(lo, count):
            return pltpu.roll(px[pl.ds(lo, count), :], hw, 1)

        def pack(rb):
            lo = pl.multiple_of(rb * half + PAD, PAD)
            first = shifted_rows(lo, hw)
            second = shifted_rows(lo + hw, hw)
            m0, m1 = first[:, :half], second[:, :half]
            for n, part in ((0, first), (1, second)):
                pm[pl.ds(lo + n * hw, hw), :] = part[:, :half]
                pe[2, pl.ds(lo + n * hw, hw), :] = part[:, half:]
            pk[1, rb, 0:hw, :] = jnp.where(low_half, m0, pltpu.roll(m1, hw, 1))
            pk[0, rb, 0:hw, :] = jnp.where(low_half, pltpu.roll(m0, hw, 1), m1)
            to_left = jnp.zeros((PAD, half), jnp.float32)
            to_right = to_left
            for k in range(half // PAD):
                part = first if k * PAD < hw else second
                q = k * PAD % hw
                e = part[q:q + PAD, half:]
                here = lane8 == k
                to_left = jnp.where(here, pltpu.roll(e, k, 1) if k else e, to_left)
                to_right = jnp.where(here, pltpu.roll(e, k + 1, 1), to_right)
            pk[0, rb, hw:hw + PAD, :] = to_left
            pk[1, rb, hw:hw + PAD, :] = to_right
            each(z_sides, lambda side, target: pk_copy(side, target, rb).start())

        ends = ((0, 0), (1, height - PAD))

        def pack_ends():
            for n, lo in ends:
                rolled = shifted_rows(lo, PAD)
                hk[n] = rolled[:, :half]
                pm[lo:lo + PAD, :] = rolled[:, :half]
                pe[2, lo:lo + PAD, :] = rolled[:, half:]
            each(z_sides, lambda side, target: hk_copy(side, target).start())

        def unpack(rb):
            each(z_sides, lambda side, target: pk_arrival(side, target, rb).wait_recv())
            lo = pl.multiple_of(rb * half + PAD, PAD)
            from_left, from_right = pr[0, rb, 0:hw, :], pr[1, rb, 0:hw, :]
            for n in range(2):
                start = lo + n * hw
                m = pm[pl.ds(start, hw), :]
                fl = pltpu.roll(from_left, hw, 1) if n else from_left
                fr = from_right if n else pltpu.roll(from_right, hw, 1)
                pe[1, pl.ds(start, hw), :] = jnp.where(low_half, fl, m)
                pe[3, pl.ds(start, hw), :] = jnp.where(low_half, m, fr)
            cl, cr = pr[0, rb, hw:hw + PAD, :], pr[1, rb, hw:hw + PAD, :]
            for k in range(half // PAD):
                pe[0, pl.ds(lo + k * PAD, PAD), :] = pltpu.roll(cl, half - 1 - k, 1)
                pe[4, pl.ds(lo + k * PAD, PAD), :] = pltpu.roll(cr, half - k, 1) if k else cr

        def unpack_ends():
            each(z_sides, lambda side, target: hk_arrival(side, target).wait_recv())
            low8 = lane8 < hw
            for n, lo in ends:
                pe[1, lo:lo + PAD, :] = jnp.where(low8, hr[0, n], hk[n])
                pe[3, lo:lo + PAD, :] = jnp.where(low8, hk[n], hr[1, n])

        lane_h = lax.broadcasted_iota(jnp.int32, (CH, half), 1)
        row_h = lax.broadcasted_iota(jnp.int32, (CH, half), 0)
        first_lane, last_lane = lane_h == 0, lane_h == half - 1

        def ahead(x):
            return pltpu.roll(x, half - 1, 1)

        def behind(x):
            return pltpu.roll(x, 1, 1)

        def weigh(rb, chosen):
            base = pl.multiple_of(rb * half + PAD, PAD)
            for r in range(0, half, CH):
                for c in chosen:
                    inner = 0 < c < strips - 1
                    mid = pe[c + 1, pl.ds(base + r, CH), :]
                    after = pm[pl.ds(base + r, CH), :] if inner else pe[c + 2, pl.ds(base + r, CH), :]
                    before = after if inner else pe[c, pl.ds(base + r, CH), :]
                    east = pe[c + 1, pl.ds(base + r + 1, CH), :]
                    west = pe[c + 1, pl.ds(base + r - 1, CH), :]
                    north = ahead(jnp.where(first_lane, after, mid))
                    south = behind(jnp.where(last_lane, before, mid))
                    se, sw, sn, ss = mid + east, mid + west, mid + north, mid + south
                    across, along = sn * ss, se * sw
                    ne, nw = east * sw * across, west * se * across
                    nn, ns = north * ss * along, south * sn * along
                    scale = coupling / jnp.maximum((ne + nw) + (nn + ns), 1e-30)
                    for n, face in enumerate((ne, nw, nn, ns)):
                        w[n, rb, c, r:r + CH, :] = face * scale

        def accumulate(store, c, value):
            store[c] = value if store[c] is None else store[c] + value

        def update(src, rb, r, part, j):
            lo = PAD + r + (half if part == 0 else 0)
            xs = [src[rb + part, j, h, lo:lo + CH, :] for h in range(2)]
            fores, afts = [ahead(x) for x in xs], [behind(x) for x in xs]
            fore = (jnp.where(last_lane, fores[1], fores[0]), jnp.where(last_lane, 0.0, fores[1]))
            aft = (jnp.where(first_lane, 0.0, afts[0]), jnp.where(first_lane, afts[0], afts[1]))
            news = []
            for h in range(2):
                c = j + h
                new = xs[h] + w[0, rb, c, r:r + CH, :] * src[rb + part, j, h, lo + 1:lo + 1 + CH, :]
                new = new + w[1, rb, c, r:r + CH, :] * src[rb + part, j, h, lo - 1:lo - 1 + CH, :]
                new = new + w[2, rb, c, r:r + CH, :] * fore[h]
                news.append(new + w[3, rb, c, r:r + CH, :] * aft[h])
            return lo, xs, news, fores[1], afts[1], fores[0], afts

        def smooth_first(rb, chosen):
            for r in range(0, half, CH):
                for c in chosen:
                    total = [None]
                    faces = [w[n, rb, c, r:r + CH, :] for n in range(4)]
                    for j, h in ((c - 1, 1), (c, 0)):
                        if not 0 <= j < ny:
                            continue
                        for part in range(2):
                            lo = PAD + r + (half if part == 0 else 0)
                            x = a[rb + part, j, h, lo:lo + CH, :]
                            beside = a[rb + part, j, 1 - h, lo:lo + CH, :]
                            fore = ahead(jnp.where(first_lane, beside if h == 0 else 0.0, x))
                            aft = behind(jnp.where(last_lane, beside if h == 1 else 0.0, x))
                            new = x + faces[0] * a[rb + part, j, h, lo + 1:lo + 1 + CH, :]
                            new = new + faces[1] * a[rb + part, j, h, lo - 1:lo - 1 + CH, :]
                            new = new + faces[2] * fore + faces[3] * aft
                            value = jnp.where(x > 0, new, 0.0)
                            b[rb + part, j, h, lo:lo + CH, :] = value
                            accumulate(total, 0, value)
                    s[rb, c, r:r + CH, :] = total[0]

        def normalise(rb):
            each(z_sides, lambda side, target: z_arrival(side, target, rb).wait_recv())
            for c in range(strips):
                for r in range(0, half, CH):
                    total = s[rb, c, r:r + CH, :]
                    if c == 0:
                        total = total + rz[0, rb, r:r + CH, :]
                    if c == strips - 1:
                        total = total + rz[1, rb, r:r + CH, :]
                    scale = 1.0 / jnp.where(total > 0, total, 1.0)
                    for z, strip in ((0, 0), (1, strips - 1)):
                        if c == strip:
                            iv[z, pl.ds(pl.multiple_of(rb * half + PAD, PAD) + r, CH), :] = scale
                    for j, h in ((c - 1, 1), (c, 0)):
                        if 0 <= j < ny:
                            for part in range(2):
                                lo = PAD + r + (half if part == 0 else 0)
                                b[rb + part, j, h, lo:lo + CH, :] = b[rb + part, j, h, lo:lo + CH, :] * scale

        row_near = lax.broadcasted_iota(jnp.int32, (NEAR, half), 0)
        lane_1 = lax.broadcasted_iota(jnp.int32, (1, half), 1)
        lane_f = lane_1.astype(jnp.float32)

        def record(rb):
            for side in range(2):
                j, strip = (0, 0) if side == 0 else (ny - 1, strips - 1)
                rim_lane = 0 if side == 0 else half - 1
                rim_row = 0 if side == 0 else NEAR - 1

                def turn(value):
                    turned = jnp.transpose(value)
                    return turned[0:NEAR] if side == 0 else turned[half - NEAR:]

                rim, places, lanes = None, [], []
                for part in range(2):
                    off = PAD + (half if part == 0 else 0)
                    inside = jnp.where(a[rb + part, j, side, PAD + half - part * PAD:PAD + half - part * PAD + 1, :] > 0, 1.0, 0.0)
                    inside = jnp.sum(inside, axis=1, keepdims=True)
                    place = (half - 1.0) - inside if side == 0 else inside
                    taken = jnp.logical_or(lane_f == (place + 1.0 if side == 0 else place - 1.0), lane_1 == rim_lane)
                    turned = turn(jnp.where(taken, b[rb + part, j, side, off:off + half, :], 0.0))
                    s[rb, strip, half + part:half + part + 1, :] = jnp.sum(
                        jnp.where(row_near == rim_row, 0.0, turned), axis=0, keepdims=True)
                    value = turned[rim_row:rim_row + 1]
                    rim = value if rim is None else rim + value
                    q = off + half - NEAR if part == 0 else off
                    beside = 1 if part == 0 else -1
                    near = b[rb + part, j, side, q:q + NEAR, :]
                    here = a[rb + part, j, side, q:q + NEAR, :]
                    over = a[rb + part, j, side, q + beside:q + beside + NEAR, :]
                    count = jnp.sum(jnp.where(here > 0, 1.0, 0.0), axis=0, keepdims=True)
                    inner = count[:, half - 1:] if side == 0 else count[:, 0:1]
                    places.append(inner + (half - NEAR) if part == 0 else (NEAR - 1) - inner)
                    lanes.append(place)
                    s[rb, strip, half + 2 + part:half + 3 + part, :] = jnp.sum(jnp.where(over > 0, 0.0, near), axis=0, keepdims=True)
                other, beside = (1, 1) if side == 0 else (ny - 2, strips - 2)
                both = b[rb, other, side, PAD + half:PAD + full, :] + b[rb + 1, other, side, PAD:PAD + half, :]
                total = s[rb, beside, 0:half, :]
                both = jnp.where(lane_1 == rim_lane, both / jnp.where(total > 0, total, 1.0), 0.0)
                s[rb, strip, half + 4:half + 5, :] = turn(both)[rim_row:rim_row + 1]
                s[rb, strip, half + 5:half + 6, :] = rim
                where = jnp.zeros((1, half), jnp.float32)
                for n, value in enumerate(places + lanes):
                    where = jnp.where(lane_1 == n, value, where)
                s[rb, strip, half + 6:half + 7, :] = where
                s[rb, strip, half + 7:, :] = jnp.zeros((1, half), jnp.float32)

        def spread(value, r):
            return jnp.sum(jnp.where(lane_h == row_h + r, value, 0.0), axis=1, keepdims=True)

        row_f = row_h.astype(jnp.float32)
        lane_hf = lane_h.astype(jnp.float32)

        def finish(rb):
            inner_up, inner_down = rb > 0, rb < nx
            base = pl.multiple_of(rb * half + PAD, PAD)

            def where_of(z, q):
                line = rz[z, q, half + 6:half + 7, :]
                return [line[:, n:n + 1] for n in range(4)]

            spots = [where_of(z, rb) for z in range(2)]
            for r in range(0, half, CH):
                lost = [None] * strips
                results = [[] for _ in range(strips)]
                for part in range(2):
                    for j in range(ny):
                        lo, xs, news, _, aft_end, fore_start, _a = update(b, rb, r, part, j)
                        for h in range(2):
                            mask = a[rb + part, j, h, lo:lo + CH, :] > 0
                            results[j + h].append((part, j, h, lo, jnp.where(mask, news[h], 0.0)))
                            accumulate(lost, j + h, jnp.where(mask, 0.0, news[h]))
                        if j + 2 < strips:
                            accumulate(lost, j + 2, w[3, rb, j + 2, r:r + CH, :] * jnp.where(first_lane, aft_end, 0.0))
                        if j >= 1:
                            accumulate(lost, j - 1, w[2, rb, j - 1, r:r + CH, :] * jnp.where(last_lane, fore_start, 0.0))
                for part, row, inner in ((0, 0, inner_up), (1, half - 1, inner_down)):
                    if r <= row < r + CH:
                        for c in range(strips):
                            over = [None]
                            for j, h, z in ((c - 1, 1, 0), (c, 0, 1)):
                                if part == 0:
                                    i, at, q = jnp.maximum(rb - 1, 0), PAD + full - 1, jnp.maximum(rb - 1, 0)
                                else:
                                    i, at, q = jnp.minimum(rb + 2, nx + 1), PAD, jnp.minimum(rb + 1, nx)
                                if 0 <= j < ny:
                                    accumulate(over, 0, b[i, j, h, at:at + 1, :])
                                else:
                                    spot = rz[z, q, half + 6:half + 7, part:part + 1]
                                    there = iv[z, pl.ds(base + (-1 if part == 0 else half), 1), :]
                                    value = rz[z, q, half + 2 + part:half + 3 + part, :] * there
                                    accumulate(over, 0, jnp.where(spot == (half if part == 0 else -1), value, 0.0))
                            keep = jnp.logical_and(row_h + r == row, inner)
                            accumulate(lost, c, w[1 - part, rb, c, r:r + CH, :] * jnp.where(keep, over[0], 0.0))
                for z, side, c in ((0, 1, 0), (1, 0, strips - 1)):
                    at_rim = last_lane if side == 0 else first_lane
                    face = 2 if side == 0 else 3
                    scale = iv[z, pl.ds(base + r, CH), :]
                    shifted = ahead(scale) if side == 0 else behind(scale)
                    v = [spread(rz[z, rb, half + n:half + n + 1, :], r) for n in (0, 1, 4, 5)]
                    field = jnp.where(lane_hf == spots[z][2], v[0], 0.0) + jnp.where(lane_hf == spots[z][3], v[1], 0.0)
                    field = field * shifted + jnp.where(at_rim, v[2], 0.0)
                    accumulate(lost, c, w[face, rb, c, r:r + CH, :] * field)
                    other = c + (1 if side == 1 else -1)
                    accumulate(lost, other, w[face, rb, other, r:r + CH, :] * jnp.where(at_rim, v[3] * shifted, 0.0))
                    for part in range(2):
                        if (r + CH > half - NEAR) if part == 0 else (r < NEAR):
                            line = jnp.where(row_f + r == spots[z][part], rz[z, rb, half + 2 + part:half + 3 + part, :], 0.0)
                            there = iv[z, pl.ds(base + r + (-1 if part == 0 else 1), CH), :]
                            accumulate(lost, c, w[1 - part, rb, c, r:r + CH, :] * line * there)
                for c in range(strips):
                    extra = ends_lost(rb, c, r)
                    total = (1.0 + coupling) - (lost[c] if extra is None else lost[c] + extra)
                    scale = 1.0 / total
                    for part, j, h, lo, value in results[c]:
                        d[rb + part, j, h, lo:lo + CH, :] = value * scale

        def ends_lost(rb, c, r):
            for end, row in ((0, 0), (1, half - 1)):
                if r <= row < r + CH:
                    keep = jnp.logical_and(row_h + r == row, rb == (0 if end == 0 else nx))
                    return w[1 - end, rb, c, r:r + CH, :] * jnp.where(keep, far[end, c, 0:1, :], 0.0)
            return None

        def gather_far():
            for end in range(2):
                at = PAD - 1 if end == 0 else 0
                for c in range(strips):
                    over = [None]
                    for j, h, z in ((c - 1, 1, 0), (c, 0, 1)):
                        accumulate(over, 0, xrow[end, j, h, at:at + 1, :] if 0 <= j < ny else zrow[z, end, at:at + 1, :])
                    far[end, c, 0:1, :] = over[0]

        def o_each(rb, act):
            for part, inside in ((0, rb > 0), (1, rb < nx)):
                @pl.when(inside)
                def _():
                    for h in range(2):
                        act(o_copy(rb, part, h))

        peers = sum(jnp.where(has, 1, 0) for _, has, _t in z_sides + x_sides)
        pl.semaphore_wait(barrier, peers)

        each(x_sides, lambda side, target: row_copy(side, target).start())

        def send_boxes(side, target):
            for h in range(2):
                g_copy(side, target, h).start()
        each(x_sides, send_boxes)
        own.wait()

        @pl.loop(0, nx + 1)
        def _(k):
            rb = pick(k, pack_order)

            @pl.when(rb == 0)
            def _():
                each(x_sides, lambda side, target: row_arrival(side, target).wait_recv())
                pack_ends()

            pack(rb)

        @pl.loop(0, nx)
        def _(i):
            a_copy(i, 0).wait()
            a_copy(i, 1).wait()

        inner_strips, outer_strips = list(range(1, strips - 1)), [0, strips - 1]

        @pl.loop(1, nx)
        def _(rb):
            weigh(rb, inner_strips)
            smooth_first(rb, inner_strips)

        for n, rb in enumerate(unpack_steps[0]):
            unpack(rb)
        unpack_ends()
        width = max(len(n) for n in unpack_steps[1:])

        @pl.loop(0, nx + 1)
        def _(k):
            rb = pick(k, weigh_order)
            for q in range(width):
                new = pick(k, [-1] + [n[q] if q < len(n) else -1 for n in unpack_steps[1:]])

                @pl.when(new >= 0)
                def _():
                    unpack(new)

            weigh(rb, outer_strips)

            @pl.when(jnp.logical_or(rb == 0, rb == nx))
            def _():
                for side, at in ((0, 0), (1, nx)):
                    @pl.when(rb == at)
                    def _():
                        _, has, target = x_sides[side]

                        @pl.when(has)
                        def _():
                            for h in range(2):
                                g_arrival(side, target, h).wait_recv()
                weigh(rb, inner_strips)
                smooth_first(rb, inner_strips)

            smooth_first(rb, outer_strips)
            record(rb)
            each(z_sides, lambda side, target: z_copy(side, target, rb).start())

        @pl.loop(0, len(events))
        def _(k):
            rb = pick(k, [n for n, _ in events])

            @pl.when(rb >= 0)
            def _():
                normalise(rb)
                for side, at in ((0, 1), (1, nx - 1)):
                    @pl.when(rb == at)
                    def _():
                        _, has, target = x_sides[side]

                        @pl.when(has)
                        def _():
                            c_copy(side, target).start()

            @pl.when(k == early)
            def _():
                def forward(end, target):
                    c_copy(end, target).wait_send()
                    c_arrival(end, target).wait_recv()
                    each(z_sides, lambda side, to: f_copy(side, to, end).start())
                each(x_sides, forward)

            now = pick(k, [n for _, n in events])

            @pl.when(k == first_end)
            def _():
                each(x_sides, lambda end, target: each(z_sides, lambda side, to: f_arrival(side, to, end).wait_recv()))
                gather_far()

            @pl.when(now >= 0)
            def _():
                finish(now)
                o_each(now, lambda copy: copy.start())

        @pl.loop(0, nx + 1)
        def _(rb):
            o_each(rb, lambda copy: copy.wait())

        def drain(side, target):
            @pl.loop(0, nx + 1)
            def _(rb):
                z_copy(side, target, rb).wait_send()
                pk_copy(side, target, rb).wait_send()
            hk_copy(side, target).wait_send()
        each(z_sides, drain)

        def drain_rows(end, target):
            row_copy(end, target).wait_send()
            for h in range(2):
                g_copy(end, target, h).wait_send()
            each(z_sides, lambda side, to: f_copy(side, to, end).wait_send())
        each(x_sides, drain_rows)

    return kernel


def local(permeability, basis, support):
    nx, ny, full, _ = basis.shape
    half = full // 2
    size_x, size_y = lax.axis_size("gx"), lax.axis_size("gy")
    height = permeability.shape[0] + half + 2 * PAD
    f32 = jnp.float32
    strips = ny + 1
    boxes = pltpu.VMEM((nx + 2, ny, 2, full + 2 * PAD, half), f32)
    scratch = [
        boxes, boxes, boxes,
        pltpu.VMEM((4, nx + 1, strips, half, half), f32),
        pltpu.VMEM((nx + 1, strips, half + PAD, half), f32),
        pltpu.VMEM((2, (nx + 1) * half + 2 * PAD, half), f32),
        pltpu.VMEM((2, nx + 1, half + PAD, half), f32),
        pltpu.VMEM((2, ny, 2, PAD, half), f32),
        pltpu.VMEM((2, 2, PAD, half), f32),
        pltpu.VMEM((2, strips, PAD, half), f32),
        pltpu.VMEM((height, full), f32),
        pltpu.VMEM((height, half), f32),
        pltpu.VMEM((strips + 2, height, half), f32),
        pltpu.VMEM((2, nx + 1, half // 2 + PAD, half), f32),
        pltpu.VMEM((2, nx + 1, half // 2 + PAD, half), f32),
        pltpu.VMEM((2, PAD, half), f32),
        pltpu.VMEM((2, 2, PAD, half), f32),
        pltpu.SemaphoreType.DMA((nx, 2)),
        pltpu.SemaphoreType.DMA,
        pltpu.SemaphoreType.DMA((nx + 1, 2, 2)),
        pltpu.SemaphoreType.DMA((2, nx + 1)),
        pltpu.SemaphoreType.DMA((2, nx + 1)),
        pltpu.SemaphoreType.DMA((2, 2)),
        pltpu.SemaphoreType.DMA((2, 2)),
        pltpu.SemaphoreType.DMA((2,)),
        pltpu.SemaphoreType.DMA((2,)),
        pltpu.SemaphoreType.DMA((2, 2)),
        pltpu.SemaphoreType.DMA((2, 2)),
        pltpu.SemaphoreType.DMA((2, nx + 1)),
        pltpu.SemaphoreType.DMA((2, nx + 1)),
        pltpu.SemaphoreType.DMA((2,)),
        pltpu.SemaphoreType.DMA((2,)),
        pltpu.SemaphoreType.DMA((2,)),
        pltpu.SemaphoreType.DMA((2,)),
    ]
    return pl.pallas_call(
        make_kernel(nx, ny, size_x, size_y, half),
        out_shape=jax.ShapeDtypeStruct(basis.shape, f32),
        in_specs=[pl.BlockSpec(memory_space=pltpu.HBM)] * 2,
        out_specs=pl.BlockSpec(memory_space=pl.ANY),
        scratch_shapes=scratch,
        compiler_params=pltpu.CompilerParams(
            collective_id=0, has_side_effects=True, vmem_limit_bytes=48 * 1024 * 1024),
        name="smoothing",
    )(*[pltpu.with_memory_space_constraint(x, pltpu.HBM) for x in (permeability, basis)])


def solution(mesh):
    placed = (P("gx", "gy"), P("gx", "gy", None, None), P("gx", "gy", None, None))
    return jax.shard_map(
        local, mesh=mesh, in_specs=placed, out_specs=P("gx", "gy", None, None), check_vma=False
    )
```

```python
import jax
import jax.numpy as jnp
from jax import lax
from jax.experimental import pallas as pl
from jax.experimental.pallas import tpu as pltpu
from jax.sharding import PartitionSpec as P

MESH = pl.DeviceIdType.MESH
relaxation = 2.0 / 3.0
coupling = relaxation / (1.0 - relaxation)
PAD = 8
CH = 64
NEAR = 40


def pick(k, table):
    value = jnp.int32(table[-1])
    for n in range(len(table) - 2, -1, -1):
        value = jnp.where(k == n, table[n], value)
    return value


def first_needs(order, count):
    seen, out = set(), []
    for rb in order:
        new = [q for q in (rb - 1, rb, rb + 1) if 0 <= q < count and q not in seen]
        seen.update(new)
        out.append(new)
    return out


def make_kernel(nx, ny, size_x, size_y, half):
    full = 2 * half
    last = nx
    strips = ny + 1
    hw = half // 2

    pack_order = [1, 2, 0, nx - 1, nx - 2, nx] + list(range(3, nx - 2))
    weigh_order = [1, nx - 1] + list(range(2, nx - 1)) + [0, nx]
    assert sorted(weigh_order) == sorted(pack_order) == list(range(nx + 1))
    unpack_steps = first_needs(weigh_order, nx + 1)
    events, done, known = [], set(), set()
    for n, rb in enumerate(weigh_order):
        known.add(rb)
        allowed = list(range(1, nx)) + ([0, nx] if n >= nx - 1 else [])
        ready = [q for q in allowed if q not in done and {m for m in (q - 1, q, q + 1) if 0 <= m <= nx} <= known][:3]
        done.update(ready)
        events += [(rb, ready[0] if ready else -1)] + [(-1, q) for q in ready[1:]]
    assert sorted(q for _, q in events if q >= 0) == list(range(nx + 1))
    first_end = min(k for k, (_, q) in enumerate(events) if q in (0, nx))
    early = [n for n, _ in events].index(3)

    def kernel(*refs):
        (perm_h, basis_h, out_h,
         a, b, d, w, s, iv, rz, xrow, zrow, far, px, pm, pe, pk, pr, hk, hr,
         a_sem, p_sem, o_sem, zs_sem, zr_sem, gs_sem, gr_sem, cs_sem, cr_sem, fs_sem, fr_sem,
         ps_sem, pr_sem, hs_sem, hr_sem, rs_sem, rr_sem) = refs
        gx, gy = lax.axis_index("gx"), lax.axis_index("gy")
        has_up, has_down = gx > 0, gx < size_x - 1
        has_left, has_right = gy > 0, gy < size_y - 1
        up, down = (gx - 1, gy), (gx + 1, gy)
        left, right = (gx, gy - 1), (gx, gy + 1)
        z_sides = ((0, has_left, left), (1, has_right, right))
        x_sides = ((0, has_up, up), (1, has_down, down))
        halo = hw + PAD
        height = px.shape[0]
        length = height - 2 * halo

        def remote(src, dst, send, recv, target):
            return pltpu.make_async_remote_copy(
                src_ref=src, dst_ref=dst, send_sem=send, recv_sem=recv, device_id=target, device_id_type=MESH)

        def a_copy(i, h):
            return pltpu.make_async_copy(
                basis_h.at[i, :, :, pl.ds(h * half, half)], a.at[i + 1, :, h, pl.ds(PAD, full), :], a_sem.at[i, h])

        def o_copy(rb, part, h):
            lo = half if part == 0 else 0
            return pltpu.make_async_copy(
                d.at[rb + part, :, h, pl.ds(PAD + lo, half), :],
                out_h.at[rb - 1 + part, :, pl.ds(lo, half), pl.ds(h * half, half)], o_sem.at[rb, part, h])

        def row_copy(side, target):
            src, dst = (0, height - halo) if side == 0 else (length - halo, 0)
            return remote(perm_h.at[pl.ds(src, halo), :], px.at[pl.ds(dst, halo), :],
                          rs_sem.at[side], rr_sem.at[1 - side], target)

        def row_arrival(side, target):
            dst = 0 if side == 0 else height - halo
            return remote(perm_h.at[pl.ds(0, halo), :], px.at[pl.ds(dst, halo), :],
                          rs_sem.at[side], rr_sem.at[side], target)

        def pk_copy(side, target, rb):
            return remote(pk.at[side, rb], pr.at[1 - side, rb], ps_sem.at[side, rb], pr_sem.at[1 - side, rb], target)

        def pk_arrival(side, target, rb):
            return remote(pk.at[side, rb], pr.at[side, rb], ps_sem.at[side, rb], pr_sem.at[side, rb], target)

        def hk_copy(side, target):
            return remote(hk, hr.at[1 - side], hs_sem.at[side], hr_sem.at[1 - side], target)

        def hk_arrival(side, target):
            return remote(hk, hr.at[side], hs_sem.at[side], hr_sem.at[side], target)

        def z_copy(side, target, rb):
            strip = 0 if side == 0 else strips - 1
            return remote(s.at[rb, strip], rz.at[1 - side, rb], zs_sem.at[side, rb], zr_sem.at[1 - side, rb], target)

        def z_arrival(side, target, rb):
            return remote(s.at[rb, 0], rz.at[side, rb], zs_sem.at[side, rb], zr_sem.at[side, rb], target)

        def g_copy(side, target, h):
            i, lo, to = (0, 0, nx + 1) if side == 0 else (nx - 1, half - PAD, 0)
            return remote(basis_h.at[i, :, pl.ds(lo, half + PAD), pl.ds(h * half, half)],
                          a.at[to, :, h, pl.ds(PAD + lo, half + PAD), :],
                          gs_sem.at[side, h], gr_sem.at[1 - side, h], target)

        def g_arrival(side, target, h):
            lo, to = (half - PAD, 0) if side == 0 else (0, nx + 1)
            return remote(basis_h.at[0, :, pl.ds(0, half + PAD), pl.ds(h * half, half)],
                          a.at[to, :, h, pl.ds(PAD + lo, half + PAD), :],
                          gs_sem.at[side, h], gr_sem.at[side, h], target)

        def c_copy(side, target):
            i, lo = (2, PAD) if side == 0 else (nx - 1, full)
            return remote(b.at[i, :, :, pl.ds(lo, PAD), :], xrow.at[1 - side], cs_sem.at[side], cr_sem.at[1 - side], target)

        def c_arrival(side, target):
            return remote(b.at[2, :, :, pl.ds(PAD, PAD), :], xrow.at[side], cs_sem.at[side], cr_sem.at[side], target)

        def f_copy(side, target, end):
            j, h = (0, 0) if side == 0 else (ny - 1, 1)
            return remote(xrow.at[end, j, h], zrow.at[1 - side, end], fs_sem.at[side, end], fr_sem.at[1 - side, end], target)

        def f_arrival(side, target, end):
            return remote(xrow.at[end, 0, 0], zrow.at[side, end], fs_sem.at[side, end], fr_sem.at[side, end], target)

        def each(sides, act):
            for side, has, target in sides:
                @pl.when(has)
                def _():
                    act(side, target)

        barrier = pltpu.get_barrier_semaphore()
        each(z_sides + x_sides, lambda side, target: pl.semaphore_signal(
            barrier, inc=1, device_id=target, device_id_type=MESH))

        own = pltpu.make_async_copy(perm_h, px.at[pl.ds(halo, length), :], p_sem)
        own.start()

        @pl.loop(0, nx)
        def _(k):
            i = pick(k, [0, nx - 1, 1, nx - 2] + list(range(2, nx - 2)))
            a_copy(i, 0).start()
            a_copy(i, 1).start()

        edge = jnp.zeros((PAD, half), jnp.float32)

        @pl.loop(0, nx)
        def _(i):
            for buf in (a, b):
                for j in range(ny):
                    for h in range(2):
                        buf[i + 1, j, h, 0:PAD, :] = edge
                        buf[i + 1, j, h, PAD + full:, :] = edge

        for buf in (a, b):
            for j in range(ny):
                for h in range(2):
                    buf[0, j, h, PAD + full:, :] = edge
                    buf[nx + 1, j, h, 0:PAD, :] = edge

        far[...] = jnp.zeros(far.shape, jnp.float32)
        for j in range(ny):
            for h in range(2):
                b[0, j, h, half:half + PAD, :] = edge
                b[nx + 1, j, h, PAD + half:2 * PAD + half, :] = edge

        for side, has, _t in z_sides:
            @pl.when(jnp.logical_not(has))
            def _():
                @pl.loop(0, nx + 1)
                def _(rb):
                    rz[side, rb] = jnp.zeros((half + PAD, half), jnp.float32)
                    pr[side, rb] = jnp.zeros((hw + PAD, half), jnp.float32)
                hr[side] = jnp.zeros((2, PAD, half), jnp.float32)
                zrow[side] = jnp.zeros((2, PAD, half), jnp.float32)

        for side, has, _t in x_sides:
            @pl.when(jnp.logical_not(has))
            def _():
                lo = 0 if side == 0 else height - halo
                px[lo:lo + halo, :] = jnp.zeros((halo, full), jnp.float32)
                lo, to = (half, 0) if side == 0 else (PAD, nx + 1)
                for j in range(ny):
                    for h in range(2):
                        a[to, j, h, lo:lo + half + PAD, :] = jnp.zeros((half + PAD, half), jnp.float32)
                xrow[side] = jnp.zeros((ny, 2, PAD, half), jnp.float32)

                for z, has_z, _z in z_sides:
                    @pl.when(has_z)
                    def _():
                        zrow[z, side] = edge

        lane = lax.broadcasted_iota(jnp.int32, (hw, half), 1)
        low_half = lane < hw
        lane8 = lax.broadcasted_iota(jnp.int32, (PAD, half), 1)

        def shifted_rows(lo, count):
            return pltpu.roll(px[pl.ds(lo, count), :], hw, 1)

        def pack(rb):
            lo = pl.multiple_of(rb * half + PAD, PAD)
            first = shifted_rows(lo, hw)
            second = shifted_rows(lo + hw, hw)
            m0, m1 = first[:, :half], second[:, :half]
            for n, part in ((0, first), (1, second)):
                pm[pl.ds(lo + n * hw, hw), :] = part[:, :half]
                pe[2, pl.ds(lo + n * hw, hw), :] = part[:, half:]
            pk[1, rb, 0:hw, :] = jnp.where(low_half, m0, pltpu.roll(m1, hw, 1))
            pk[0, rb, 0:hw, :] = jnp.where(low_half, pltpu.roll(m0, hw, 1), m1)
            to_left = jnp.zeros((PAD, half), jnp.float32)
            to_right = to_left
            for k in range(half // PAD):
                part = first if k * PAD < hw else second
                q = k * PAD % hw
                e = part[q:q + PAD, half:]
                here = lane8 == k
                to_left = jnp.where(here, pltpu.roll(e, k, 1) if k else e, to_left)
                to_right = jnp.where(here, pltpu.roll(e, k + 1, 1), to_right)
            pk[0, rb, hw:hw + PAD, :] = to_left
            pk[1, rb, hw:hw + PAD, :] = to_right
            each(z_sides, lambda side, target: pk_copy(side, target, rb).start())

        ends = ((0, 0), (1, height - PAD))

        def pack_ends():
            for n, lo in ends:
                rolled = shifted_rows(lo, PAD)
                hk[n] = rolled[:, :half]
                pm[lo:lo + PAD, :] = rolled[:, :half]
                pe[2, lo:lo + PAD, :] = rolled[:, half:]
            each(z_sides, lambda side, target: hk_copy(side, target).start())

        def unpack(rb):
            each(z_sides, lambda side, target: pk_arrival(side, target, rb).wait_recv())
            lo = pl.multiple_of(rb * half + PAD, PAD)
            from_left, from_right = pr[0, rb, 0:hw, :], pr[1, rb, 0:hw, :]
            for n in range(2):
                start = lo + n * hw
                m = pm[pl.ds(start, hw), :]
                fl = pltpu.roll(from_left, hw, 1) if n else from_left
                fr = from_right if n else pltpu.roll(from_right, hw, 1)
                pe[1, pl.ds(start, hw), :] = jnp.where(low_half, fl, m)
                pe[3, pl.ds(start, hw), :] = jnp.where(low_half, m, fr)
            cl, cr = pr[0, rb, hw:hw + PAD, :], pr[1, rb, hw:hw + PAD, :]
            for k in range(half // PAD):
                pe[0, pl.ds(lo + k * PAD, PAD), :] = pltpu.roll(cl, half - 1 - k, 1)
                pe[4, pl.ds(lo + k * PAD, PAD), :] = pltpu.roll(cr, half - k, 1) if k else cr

        def unpack_ends():
            each(z_sides, lambda side, target: hk_arrival(side, target).wait_recv())
            low8 = lane8 < hw
            for n, lo in ends:
                pe[1, lo:lo + PAD, :] = jnp.where(low8, hr[0, n], hk[n])
                pe[3, lo:lo + PAD, :] = jnp.where(low8, hk[n], hr[1, n])

        lane_h = lax.broadcasted_iota(jnp.int32, (CH, half), 1)
        row_h = lax.broadcasted_iota(jnp.int32, (CH, half), 0)
        first_lane, last_lane = lane_h == 0, lane_h == half - 1

        def ahead(x):
            return pltpu.roll(x, half - 1, 1)

        def behind(x):
            return pltpu.roll(x, 1, 1)

        def weigh(rb, chosen):
            base = pl.multiple_of(rb * half + PAD, PAD)
            for r in range(0, half, CH):
                for c in chosen:
                    inner = 0 < c < strips - 1
                    mid = pe[c + 1, pl.ds(base + r, CH), :]
                    after = pm[pl.ds(base + r, CH), :] if inner else pe[c + 2, pl.ds(base + r, CH), :]
                    before = after if inner else pe[c, pl.ds(base + r, CH), :]
                    east = pe[c + 1, pl.ds(base + r + 1, CH), :]
                    west = pe[c + 1, pl.ds(base + r - 1, CH), :]
                    north = ahead(jnp.where(first_lane, after, mid))
                    south = behind(jnp.where(last_lane, before, mid))
                    se, sw, sn, ss = mid + east, mid + west, mid + north, mid + south
                    across, along = sn * ss, se * sw
                    ne, nw = east * sw * across, west * se * across
                    nn, ns = north * ss * along, south * sn * along
                    scale = coupling / jnp.maximum((ne + nw) + (nn + ns), 1e-30)
                    for n, face in enumerate((ne, nw, nn, ns)):
                        w[n, rb, c, r:r + CH, :] = face * scale

        def accumulate(store, c, value):
            store[c] = value if store[c] is None else store[c] + value

        def update(src, rb, r, part, j):
            lo = PAD + r + (half if part == 0 else 0)
            xs = [src[rb + part, j, h, lo:lo + CH, :] for h in range(2)]
            fores, afts = [ahead(x) for x in xs], [behind(x) for x in xs]
            fore = (jnp.where(last_lane, fores[1], fores[0]), jnp.where(last_lane, 0.0, fores[1]))
            aft = (jnp.where(first_lane, 0.0, afts[0]), jnp.where(first_lane, afts[0], afts[1]))
            news = []
            for h in range(2):
                c = j + h
                new = xs[h] + w[0, rb, c, r:r + CH, :] * src[rb + part, j, h, lo + 1:lo + 1 + CH, :]
                new = new + w[1, rb, c, r:r + CH, :] * src[rb + part, j, h, lo - 1:lo - 1 + CH, :]
                new = new + w[2, rb, c, r:r + CH, :] * fore[h]
                news.append(new + w[3, rb, c, r:r + CH, :] * aft[h])
            return lo, xs, news, fores[1], afts[1], fores[0], afts

        def smooth_first(rb, chosen):
            for r in range(0, half, CH):
                for c in chosen:
                    total = [None]
                    faces = [w[n, rb, c, r:r + CH, :] for n in range(4)]
                    for j, h in ((c - 1, 1), (c, 0)):
                        if not 0 <= j < ny:
                            continue
                        for part in range(2):
                            lo = PAD + r + (half if part == 0 else 0)
                            x = a[rb + part, j, h, lo:lo + CH, :]
                            beside = a[rb + part, j, 1 - h, lo:lo + CH, :]
                            fore = ahead(jnp.where(first_lane, beside if h == 0 else 0.0, x))
                            aft = behind(jnp.where(last_lane, beside if h == 1 else 0.0, x))
                            new = x + faces[0] * a[rb + part, j, h, lo + 1:lo + 1 + CH, :]
                            new = new + faces[1] * a[rb + part, j, h, lo - 1:lo - 1 + CH, :]
                            new = new + faces[2] * fore + faces[3] * aft
                            value = jnp.where(x > 0, new, 0.0)
                            b[rb + part, j, h, lo:lo + CH, :] = value
                            accumulate(total, 0, value)
                    s[rb, c, r:r + CH, :] = total[0]

        def normalise(rb, chosen):
            for c in chosen:
                for r in range(0, half, CH):
                    total = s[rb, c, r:r + CH, :]
                    if c == 0:
                        total = total + rz[0, rb, r:r + CH, :]
                    if c == strips - 1:
                        total = total + rz[1, rb, r:r + CH, :]
                    scale = 1.0 / jnp.where(total > 0, total, 1.0)
                    for z, strip in ((0, 0), (1, strips - 1)):
                        if c == strip:
                            iv[z, pl.ds(pl.multiple_of(rb * half + PAD, PAD) + r, CH), :] = scale
                    for j, h in ((c - 1, 1), (c, 0)):
                        if 0 <= j < ny:
                            for part in range(2):
                                lo = PAD + r + (half if part == 0 else 0)
                                b[rb + part, j, h, lo:lo + CH, :] = b[rb + part, j, h, lo:lo + CH, :] * scale

        row_near = lax.broadcasted_iota(jnp.int32, (NEAR, half), 0)
        lane_1 = lax.broadcasted_iota(jnp.int32, (1, half), 1)
        lane_f = lane_1.astype(jnp.float32)

        def record(rb):
            for side in range(2):
                j, strip = (0, 0) if side == 0 else (ny - 1, strips - 1)
                rim_lane = 0 if side == 0 else half - 1
                rim_row = 0 if side == 0 else NEAR - 1

                def turn(value):
                    turned = jnp.transpose(value)
                    return turned[0:NEAR] if side == 0 else turned[half - NEAR:]

                rim, places, lanes = None, [], []
                for part in range(2):
                    off = PAD + (half if part == 0 else 0)
                    inside = jnp.where(a[rb + part, j, side, PAD + half - part * PAD:PAD + half - part * PAD + 1, :] > 0, 1.0, 0.0)
                    inside = jnp.sum(inside, axis=1, keepdims=True)
                    place = (half - 1.0) - inside if side == 0 else inside
                    taken = jnp.logical_or(lane_f == (place + 1.0 if side == 0 else place - 1.0), lane_1 == rim_lane)
                    turned = turn(jnp.where(taken, b[rb + part, j, side, off:off + half, :], 0.0))
                    s[rb, strip, half + part:half + part + 1, :] = jnp.sum(
                        jnp.where(row_near == rim_row, 0.0, turned), axis=0, keepdims=True)
                    value = turned[rim_row:rim_row + 1]
                    rim = value if rim is None else rim + value
                    q = off + half - NEAR if part == 0 else off
                    beside = 1 if part == 0 else -1
                    near = b[rb + part, j, side, q:q + NEAR, :]
                    here = a[rb + part, j, side, q:q + NEAR, :]
                    over = a[rb + part, j, side, q + beside:q + beside + NEAR, :]
                    count = jnp.sum(jnp.where(here > 0, 1.0, 0.0), axis=0, keepdims=True)
                    inner = count[:, half - 1:] if side == 0 else count[:, 0:1]
                    places.append(inner + (half - NEAR) if part == 0 else (NEAR - 1) - inner)
                    lanes.append(place)
                    s[rb, strip, half + 2 + part:half + 3 + part, :] = jnp.sum(jnp.where(over > 0, 0.0, near), axis=0, keepdims=True)
                other, beside = (1, 1) if side == 0 else (ny - 2, strips - 2)
                both = b[rb, other, side, PAD + half:PAD + full, :] + b[rb + 1, other, side, PAD:PAD + half, :]
                total = s[rb, beside, 0:half, :]
                both = jnp.where(lane_1 == rim_lane, both / jnp.where(total > 0, total, 1.0), 0.0)
                s[rb, strip, half + 4:half + 5, :] = turn(both)[rim_row:rim_row + 1]
                s[rb, strip, half + 5:half + 6, :] = rim
                where = jnp.zeros((1, half), jnp.float32)
                for n, value in enumerate(places + lanes):
                    where = jnp.where(lane_1 == n, value, where)
                s[rb, strip, half + 6:half + 7, :] = where
                s[rb, strip, half + 7:, :] = jnp.zeros((1, half), jnp.float32)

        def spread(value, r):
            return jnp.sum(jnp.where(lane_h == row_h + r, value, 0.0), axis=1, keepdims=True)

        row_f = row_h.astype(jnp.float32)
        lane_hf = lane_h.astype(jnp.float32)

        def finish(rb):
            inner_up, inner_down = rb > 0, rb < nx
            base = pl.multiple_of(rb * half + PAD, PAD)

            def where_of(z, q):
                line = rz[z, q, half + 6:half + 7, :]
                return [line[:, n:n + 1] for n in range(4)]

            spots = [where_of(z, rb) for z in range(2)]
            for r in range(0, half, CH):
                lost = [None] * strips
                results = [[] for _ in range(strips)]
                for part in range(2):
                    for j in range(ny):
                        lo, xs, news, _, aft_end, fore_start, _a = update(b, rb, r, part, j)
                        for h in range(2):
                            mask = a[rb + part, j, h, lo:lo + CH, :] > 0
                            results[j + h].append((part, j, h, lo, jnp.where(mask, news[h], 0.0)))
                            accumulate(lost, j + h, jnp.where(mask, 0.0, news[h]))
                        if j + 2 < strips:
                            accumulate(lost, j + 2, w[3, rb, j + 2, r:r + CH, :] * jnp.where(first_lane, aft_end, 0.0))
                        if j >= 1:
                            accumulate(lost, j - 1, w[2, rb, j - 1, r:r + CH, :] * jnp.where(last_lane, fore_start, 0.0))
                for part, row, inner in ((0, 0, inner_up), (1, half - 1, inner_down)):
                    if r <= row < r + CH:
                        for c in range(strips):
                            over = [None]
                            for j, h, z in ((c - 1, 1, 0), (c, 0, 1)):
                                if part == 0:
                                    i, at, q = jnp.maximum(rb - 1, 0), PAD + full - 1, jnp.maximum(rb - 1, 0)
                                else:
                                    i, at, q = jnp.minimum(rb + 2, nx + 1), PAD, jnp.minimum(rb + 1, nx)
                                if 0 <= j < ny:
                                    accumulate(over, 0, b[i, j, h, at:at + 1, :])
                                else:
                                    spot = rz[z, q, half + 6:half + 7, part:part + 1]
                                    there = iv[z, pl.ds(base + (-1 if part == 0 else half), 1), :]
                                    value = rz[z, q, half + 2 + part:half + 3 + part, :] * there
                                    accumulate(over, 0, jnp.where(spot == (half if part == 0 else -1), value, 0.0))
                            keep = jnp.logical_and(row_h + r == row, inner)
                            accumulate(lost, c, w[1 - part, rb, c, r:r + CH, :] * jnp.where(keep, over[0], 0.0))
                for z, side, c in ((0, 1, 0), (1, 0, strips - 1)):
                    at_rim = last_lane if side == 0 else first_lane
                    face = 2 if side == 0 else 3
                    scale = iv[z, pl.ds(base + r, CH), :]
                    shifted = ahead(scale) if side == 0 else behind(scale)
                    v = [spread(rz[z, rb, half + n:half + n + 1, :], r) for n in (0, 1, 4, 5)]
                    field = jnp.where(lane_hf == spots[z][2], v[0], 0.0) + jnp.where(lane_hf == spots[z][3], v[1], 0.0)
                    field = field * shifted + jnp.where(at_rim, v[2], 0.0)
                    accumulate(lost, c, w[face, rb, c, r:r + CH, :] * field)
                    other = c + (1 if side == 1 else -1)
                    accumulate(lost, other, w[face, rb, other, r:r + CH, :] * jnp.where(at_rim, v[3] * shifted, 0.0))
                    for part in range(2):
                        if (r + CH > half - NEAR) if part == 0 else (r < NEAR):
                            line = jnp.where(row_f + r == spots[z][part], rz[z, rb, half + 2 + part:half + 3 + part, :], 0.0)
                            there = iv[z, pl.ds(base + r + (-1 if part == 0 else 1), CH), :]
                            accumulate(lost, c, w[1 - part, rb, c, r:r + CH, :] * line * there)
                for c in range(strips):
                    extra = ends_lost(rb, c, r)
                    total = (1.0 + coupling) - (lost[c] if extra is None else lost[c] + extra)
                    scale = 1.0 / total
                    for part, j, h, lo, value in results[c]:
                        d[rb + part, j, h, lo:lo + CH, :] = value * scale

        def ends_lost(rb, c, r):
            for end, row in ((0, 0), (1, half - 1)):
                if r <= row < r + CH:
                    keep = jnp.logical_and(row_h + r == row, rb == (0 if end == 0 else nx))
                    return w[1 - end, rb, c, r:r + CH, :] * jnp.where(keep, far[end, c, 0:1, :], 0.0)
            return None

        def gather_far():
            for end in range(2):
                at = PAD - 1 if end == 0 else 0
                for c in range(strips):
                    over = [None]
                    for j, h, z in ((c - 1, 1, 0), (c, 0, 1)):
                        accumulate(over, 0, xrow[end, j, h, at:at + 1, :] if 0 <= j < ny else zrow[z, end, at:at + 1, :])
                    far[end, c, 0:1, :] = over[0]

        def o_each(rb, act):
            for part, inside in ((0, rb > 0), (1, rb < nx)):
                @pl.when(inside)
                def _():
                    for h in range(2):
                        act(o_copy(rb, part, h))

        peers = sum(jnp.where(has, 1, 0) for _, has, _t in z_sides + x_sides)
        pl.semaphore_wait(barrier, peers)

        each(x_sides, lambda side, target: row_copy(side, target).start())

        def send_boxes(side, target):
            for h in range(2):
                g_copy(side, target, h).start()
        each(x_sides, send_boxes)
        own.wait()

        @pl.loop(0, nx + 1)
        def _(k):
            rb = pick(k, pack_order)

            @pl.when(rb == 0)
            def _():
                each(x_sides, lambda side, target: row_arrival(side, target).wait_recv())
                pack_ends()

            pack(rb)

        @pl.loop(0, nx)
        def _(i):
            a_copy(i, 0).wait()
            a_copy(i, 1).wait()

        inner_strips, outer_strips = list(range(1, strips - 1)), [0, strips - 1]

        @pl.loop(1, nx)
        def _(rb):
            weigh(rb, inner_strips)
            smooth_first(rb, inner_strips)

        for n, rb in enumerate(unpack_steps[0]):
            unpack(rb)
        unpack_ends()
        width = max(len(n) for n in unpack_steps[1:])

        @pl.loop(0, nx + 1)
        def _(k):
            rb = pick(k, weigh_order)
            for q in range(width):
                new = pick(k, [-1] + [n[q] if q < len(n) else -1 for n in unpack_steps[1:]])

                @pl.when(new >= 0)
                def _():
                    unpack(new)

            weigh(rb, outer_strips)

            @pl.when(jnp.logical_or(rb == 0, rb == nx))
            def _():
                for side, at in ((0, 0), (1, nx)):
                    @pl.when(rb == at)
                    def _():
                        _, has, target = x_sides[side]

                        @pl.when(has)
                        def _():
                            for h in range(2):
                                g_arrival(side, target, h).wait_recv()
                weigh(rb, inner_strips)
                smooth_first(rb, inner_strips)

            smooth_first(rb, outer_strips)
            record(rb)
            each(z_sides, lambda side, target: z_copy(side, target, rb).start())
            normalise(rb, inner_strips)

        @pl.loop(0, len(events))
        def _(k):
            rb = pick(k, [n for n, _ in events])

            @pl.when(rb >= 0)
            def _():
                each(z_sides, lambda side, target: z_arrival(side, target, rb).wait_recv())
                normalise(rb, outer_strips)
                for side, at in ((0, 1), (1, nx - 1)):
                    @pl.when(rb == at)
                    def _():
                        _, has, target = x_sides[side]

                        @pl.when(has)
                        def _():
                            c_copy(side, target).start()

            @pl.when(k == early)
            def _():
                def forward(end, target):
                    c_copy(end, target).wait_send()
                    c_arrival(end, target).wait_recv()
                    each(z_sides, lambda side, to: f_copy(side, to, end).start())
                each(x_sides, forward)

            now = pick(k, [n for _, n in events])

            @pl.when(k == first_end)
            def _():
                each(x_sides, lambda end, target: each(z_sides, lambda side, to: f_arrival(side, to, end).wait_recv()))
                gather_far()

            @pl.when(now >= 0)
            def _():
                finish(now)
                o_each(now, lambda copy: copy.start())

        @pl.loop(0, nx + 1)
        def _(rb):
            o_each(rb, lambda copy: copy.wait())

        def drain(side, target):
            @pl.loop(0, nx + 1)
            def _(rb):
                z_copy(side, target, rb).wait_send()
                pk_copy(side, target, rb).wait_send()
            hk_copy(side, target).wait_send()
        each(z_sides, drain)

        def drain_rows(end, target):
            row_copy(end, target).wait_send()
            for h in range(2):
                g_copy(end, target, h).wait_send()
            each(z_sides, lambda side, to: f_copy(side, to, end).wait_send())
        each(x_sides, drain_rows)

    return kernel


def local(permeability, basis, support):
    nx, ny, full, _ = basis.shape
    half = full // 2
    size_x, size_y = lax.axis_size("gx"), lax.axis_size("gy")
    height = permeability.shape[0] + half + 2 * PAD
    f32 = jnp.float32
    strips = ny + 1
    boxes = pltpu.VMEM((nx + 2, ny, 2, full + 2 * PAD, half), f32)
    scratch = [
        boxes, boxes, boxes,
        pltpu.VMEM((4, nx + 1, strips, half, half), f32),
        pltpu.VMEM((nx + 1, strips, half + PAD, half), f32),
        pltpu.VMEM((2, (nx + 1) * half + 2 * PAD, half), f32),
        pltpu.VMEM((2, nx + 1, half + PAD, half), f32),
        pltpu.VMEM((2, ny, 2, PAD, half), f32),
        pltpu.VMEM((2, 2, PAD, half), f32),
        pltpu.VMEM((2, strips, PAD, half), f32),
        pltpu.VMEM((height, full), f32),
        pltpu.VMEM((height, half), f32),
        pltpu.VMEM((strips + 2, height, half), f32),
        pltpu.VMEM((2, nx + 1, half // 2 + PAD, half), f32),
        pltpu.VMEM((2, nx + 1, half // 2 + PAD, half), f32),
        pltpu.VMEM((2, PAD, half), f32),
        pltpu.VMEM((2, 2, PAD, half), f32),
        pltpu.SemaphoreType.DMA((nx, 2)),
        pltpu.SemaphoreType.DMA,
        pltpu.SemaphoreType.DMA((nx + 1, 2, 2)),
        pltpu.SemaphoreType.DMA((2, nx + 1)),
        pltpu.SemaphoreType.DMA((2, nx + 1)),
        pltpu.SemaphoreType.DMA((2, 2)),
        pltpu.SemaphoreType.DMA((2, 2)),
        pltpu.SemaphoreType.DMA((2,)),
        pltpu.SemaphoreType.DMA((2,)),
        pltpu.SemaphoreType.DMA((2, 2)),
        pltpu.SemaphoreType.DMA((2, 2)),
        pltpu.SemaphoreType.DMA((2, nx + 1)),
        pltpu.SemaphoreType.DMA((2, nx + 1)),
        pltpu.SemaphoreType.DMA((2,)),
        pltpu.SemaphoreType.DMA((2,)),
        pltpu.SemaphoreType.DMA((2,)),
        pltpu.SemaphoreType.DMA((2,)),
    ]
    return pl.pallas_call(
        make_kernel(nx, ny, size_x, size_y, half),
        out_shape=jax.ShapeDtypeStruct(basis.shape, f32),
        in_specs=[pl.BlockSpec(memory_space=pltpu.HBM)] * 2,
        out_specs=pl.BlockSpec(memory_space=pl.ANY),
        scratch_shapes=scratch,
        compiler_params=pltpu.CompilerParams(
            collective_id=0, has_side_effects=True, vmem_limit_bytes=48 * 1024 * 1024),
        name="smoothing",
    )(*[pltpu.with_memory_space_constraint(x, pltpu.HBM) for x in (permeability, basis)])


def solution(mesh):
    placed = (P("gx", "gy"), P("gx", "gy", None, None), P("gx", "gy", None, None))
    return jax.shard_map(
        local, mesh=mesh, in_specs=placed, out_specs=P("gx", "gy", None, None), check_vma=False
    )
```
